256 devices in a mesh: gx: 4 (over y_hi, core), gy: 8 (over z), gz: 8 (over y_lo, x).
Axes of the slice: x: 4, y: 4 (y_hi: 2, y_lo: 2; y = y_hi * 2 + y_lo), z: 8, core: 2. Of those that a mesh axis runs over, the one named last changes fastest.
Arguments:
- order_param: float32 [16, 128, 1024], P('gx', 'gy', 'gz'), may hold values from -1 to 1
- density: float32 [16, 128, 1024], P('gx', 'gy', 'gz'), may hold values from 0.7 to 1.3
- velocity: float32 [3, 16, 128, 1024], P(None, 'gx', 'gy', 'gz'), may hold values from -0.3 to 0.3
Outputs:
- final_order: float32 [16, 128, 1024], P('gx', 'gy', 'gz')
- populations: float32 [19, 16, 128, 1024], P(None, 'gx', 'gy', 'gz')
The draws below stay inside these ranges and needn't reach their ends.
All inputs are finite; a program needn't handle non-finite values.
Results may differ from the reference program's by a relative error of at most 0.0001.
Values sent between devices are 32-bit elements; how exact they have to be, the bound alone decides.
No kernel may reach another device: no remote copies, remote signals or barrier semaphores. Data moves between devices by JAX's collectives and lax.ppermute only.
A program may use at most 64 MiB of HBM per device.

```python
import jax
import jax.numpy as jnp

ITERS = 5
NX = 16
NY = 128
NZ = 1024


def block_scale(rng, extent, shards, smallest, top_value):
    factor_of, own = 1.0, jax.random.fold_in(rng, 6)
    for dim, shards_of in shards:
        draws = jnp.exp(jax.random.uniform(jax.random.fold_in(own, dim), (shards_of,), jnp.float32, smallest / len(shards), top_value / len(shards)))
        factor_of = factor_of * jnp.repeat(draws, extent[dim] // shards_of).reshape([-1 if axis == dim else 1 for axis in range(len(extent))])
    return factor_of


def bell_draw(rng, shape, deviation, reach, split=(), held_as=jnp.bfloat16):
    entries = jax.random.normal(rng, shape, jnp.float32) * deviation
    if len(split) > 0:
        entries = block_scale(rng, shape, split, -0.22, 0.18) * entries
    return jnp.clip(entries, min=-reach, max=reach).astype(held_as)


def setup_inputs(seed: int = 0) -> dict:
    seeds = jax.random.split(jax.random.key(seed), 4)
    return {
        "order_param": jnp.clip(jax.random.uniform(seeds[0], (NX, NY, NZ), jnp.float32, -1.0, 1.0) * block_scale(seeds[0], (NX, NY, NZ), ((0, 4), (1, 8), (2, 8)), -0.4, 0.0), -1.0, 1.0),
        "density": jnp.clip(0.7 + 0.59999996 * jax.random.uniform(seeds[1], (NX, NY, NZ), jnp.float32) ** block_scale(seeds[1], (NX, NY, NZ), ((0, 4), (1, 8), (2, 8)), -0.2, 0.2), 0.7, 1.3),
        "velocity": bell_draw(seeds[2], (3, NX, NY, NZ), 0.1, 0.3, ((1, 4), (2, 8), (3, 8)), jnp.float32),
    }


DIRECTIONS = [(0, 0, 0), (1, 0, 0), (-1, 0, 0), (0, 1, 0), (0, -1, 0), (0, 0, 1), (0, 0, -1),
              (1, 1, 0), (-1, -1, 0), (1, -1, 0), (-1, 1, 0), (1, 0, 1), (-1, 0, -1), (1, 0, -1),
              (-1, 0, 1), (0, 1, 1), (0, -1, -1), (0, 1, -1), (0, -1, 1)]
WEIGHTS = [1.0 / 3.0] + [1.0 / 18.0] * 6 + [1.0 / 36.0] * 12
quadratic = -0.1
quartic = 0.1
stiffness = 0.02
mobility = 0.5
relax_time = 0.8


def equilibrium(dens, flow):
    usq = flow[0] * flow[0] + flow[1] * flow[1] + flow[2] * flow[2]
    out = []
    for i in range(19):
        along = jnp.zeros_like(dens)
        for d in range(3):
            if DIRECTIONS[i][d] != 0:
                along = along + DIRECTIONS[i][d] * flow[d]
        out.append(WEIGHTS[i] * dens * (1.0 + 3.0 * along + 4.5 * along * along - 1.5 * usq))
    return jnp.stack(out)


def moments(pops):
    dens = jnp.sum(pops, axis=0)
    moms = []
    for d in range(3):
        total = jnp.zeros_like(dens)
        for i in range(19):
            if DIRECTIONS[i][d] == 1:
                total = total + pops[i]
            elif DIRECTIONS[i][d] == -1:
                total = total - pops[i]
        moms.append(total)
    return dens, jnp.stack(moms)


def reference(order_param, density, velocity):
    order = order_param
    pops = equilibrium(density, velocity)
    for step in range(ITERS):
        beside = -6.0 * order
        for d in range(3):
            beside = beside + jnp.roll(order, 1, d) + jnp.roll(order, -1, d)
        chem = quadratic * order + quartic * order * order * order - stiffness * beside
        force = jnp.stack([-order * (jnp.roll(chem, -1, d) - jnp.roll(chem, 1, d)) * 0.5 for d in range(3)])
        dens, moms = moments(pops)
        vel = moms / dens
        base = equilibrium(dens, vel)
        moved = equilibrium(dens, vel + force / dens)
        post = pops - (pops - base) / relax_time + moved - base
        pops = jnp.stack([jnp.roll(post[i], DIRECTIONS[i], (0, 1, 2)) for i in range(19)])
        dens2, moms2 = moments(pops)
        flow = moms2 / dens2
        change = jnp.zeros_like(order)
        for d in range(3):
            flux = 0.25 * (flow[d] + jnp.roll(flow[d], -1, d)) * (order + jnp.roll(order, -1, d)) - mobility * (jnp.roll(chem, -1, d) - chem)
            change = change + flux - jnp.roll(flux, 1, d)
        order = order - change
    return order, pops
```

```python
import jax
import jax.numpy as jnp
from jax import lax
from jax.experimental import pallas as pl
from jax.experimental.pallas import tpu as pltpu
from jax.sharding import PartitionSpec as P

ITERS = 5
DIRECTIONS = [
    (0, 0, 0),
    (1, 0, 0),
    (-1, 0, 0),
    (0, 1, 0),
    (0, -1, 0),
    (0, 0, 1),
    (0, 0, -1),
    (1, 1, 0),
    (-1, -1, 0),
    (1, -1, 0),
    (-1, 1, 0),
    (1, 0, 1),
    (-1, 0, -1),
    (1, 0, -1),
    (-1, 0, 1),
    (0, 1, 1),
    (0, -1, -1),
    (0, 1, -1),
    (0, -1, 1),
]
INDEX = {c: i for i, c in enumerate(DIRECTIONS)}
quadratic = -0.1
quartic = 0.1
stiffness = 0.02
mobility = 0.5

AXES = ("gx", "gy", "gz")
F32 = jnp.float32
NX = 16
BY = 16
LANES = 128
EDGE = 20
GAP = 24
ROWS = 80
OWN = 30


def tiles(radius):
    low = (OWN - radius) // 8 * 8
    high = -(-(OWN + BY + radius) // 8) * 8
    return list(range(low, high, 8))


def lane_masks(core, shape):
    lane = lax.broadcasted_iota(jnp.int32, shape, len(shape) - 1)
    low, high = lane < EDGE, lane >= LANES - EDGE
    first = core == 0
    send = (first & low) | (jnp.logical_not(first) & high)
    take = (first & high) | (jnp.logical_not(first) & low)
    return send, take


def gather_pair(core_ref, mine_ref, other_ref, both_ref, edge_ref):
    core = core_ref[0]
    lo, hi = core * 4, 4 - core * 4
    send, _ = lane_masks(core, (BY, LANES))
    for source, base in ((mine_ref, lo), (other_ref, hi)):
        for x in range(4):
            packed = None
            for f in range(5):
                value = source[f, x]
                both_ref[f, base + x] = value
                part = jnp.where(send, value, 0.0)
                part = pltpu.roll(part, GAP * f, 1) if f else part
                packed = part if packed is None else packed + part
            edge_ref[base + x] = packed


def merge_edges(core_ref, near_ref, far_ref, near_edge, far_edge, out_ref, up_ref, down_ref):
    _, take = lane_masks(core_ref[0], (BY, LANES))
    for x in range(NX):
        source, edges = (near_ref, near_edge) if x < 8 else (far_ref, far_edge)
        edge = edges[x % 8]
        row = (x % 2) * 12
        for f in range(5):
            moved = pltpu.roll(edge, LANES - GAP * f, 1) if f else edge
            value = jnp.where(take, moved, source[f, x % 8])
            out_ref[f, x] = value
            count = 4 if f == 0 else 2
            up_ref[x // 2, row : row + count, :] = value[BY - count :]
            down_ref[x // 2, row : row + count, :] = value[:count]
            row += count


def prev_lane(v):
    return pltpu.roll(v, 1, 1)


def next_lane(v):
    return pltpu.roll(v, LANES - 1, 1)


def collide(rho, vel, kick, old):
    moved = [v + g for v, g in zip(vel, kick)]
    pairs = ((0, 1), (0, 2), (1, 2))
    unit = rho * (1.0 / 36.0)
    if old is None:
        square = [m * m for m in moved]
        cross = [moved[d] * moved[e] for d, e in pairs]
        drift = moved
        rest = 1.0
    else:
        square = [0.25 * (v * v) + m * m for v, m in zip(vel, moved)]
        cross = [0.25 * (vel[d] * vel[e]) + moved[d] * moved[e] for d, e in pairs]
        drift = [1.25 * v + g for v, g in zip(vel, kick)]
        rest = 1.25
    base = unit * (rest - 1.5 * (square[0] + square[1] + square[2]))
    unit45 = unit * 4.5
    unit9 = unit * 9.0
    unit3 = unit * 3.0
    sq = [unit45 * s for s in square]
    cr = [unit9 * q for q in cross]
    dr = [unit3 * b for b in drift]

    def settle(i, value):
        return value if old is None else value - 0.25 * old(i)

    post = {0: settle(0, 12.0 * base)}
    for d in range(3):
        even = 2.0 * (base + sq[d])
        odd = 2.0 * dr[d]
        c = [0, 0, 0]
        c[d] = 1
        i = INDEX[tuple(c)]
        post[i] = settle(i, even + odd)
        c[d] = -1
        i = INDEX[tuple(c)]
        post[i] = settle(i, even - odd)
    for k, (d, e) in enumerate(pairs):
        even = base + (sq[d] + sq[e])
        for sign in (1, -1):
            part = even + cr[k] if sign == 1 else even - cr[k]
            odd = dr[d] + dr[e] if sign == 1 else dr[d] - dr[e]
            c = [0, 0, 0]
            c[d], c[e] = 1, sign
            i = INDEX[tuple(c)]
            post[i] = settle(i, part + odd)
            c[d], c[e] = -1, -sign
            i = INDEX[tuple(c)]
            post[i] = settle(i, part - odd)
    return post


def moments(f):
    both, diff = {}, {}
    for i in range(1, 19, 2):
        both[i] = f[i] + f[i + 1]
        diff[i] = f[i] - f[i + 1]
    rho = ((f[0] + both[1]) + (both[3] + both[5])) + (
        ((both[7] + both[9]) + (both[11] + both[13])) + (both[15] + both[17])
    )
    mx = (diff[1] + (diff[7] + diff[9])) + (diff[11] + diff[13])
    my = (diff[3] + (diff[7] - diff[9])) + (diff[15] + diff[17])
    mz = (diff[5] + (diff[11] - diff[13])) + (diff[15] - diff[17])
    return rho, (mx, my, mz)


def steps_kernel(core_ref, own, low, high, low2, high2, mine_ref, send_ref, pops_a, pops_b, order_a, order_b, chem, rho, inv, vel):
    core = core_ref[0]

    def load(x, _):
        odd = lax.rem(x, 2)
        pair = lax.div(x, 2)
        for f, target in enumerate((order_a, rho, vel.at[0], vel.at[1], vel.at[2])):
            target[x, pl.ds(OWN - 16, 16), :] = low[f, x]
            target[x, pl.ds(OWN, 16), :] = own[f, x]
            target[x, pl.ds(OWN + 16, 16), :] = high[f, x]
            count = 4 if f == 0 else 2
            row = 0 if f == 0 else 2 + 2 * f
            for half in range(2):

                @pl.when(odd == half)
                def _():
                    target[x, pl.ds(OWN - 16 - count, count), :] = low2[pair, half * 12 + row : half * 12 + row + count, :]
                    target[x, pl.ds(OWN + 32, count), :] = high2[pair, half * 12 + row : half * 12 + row + count, :]
        return 0

    lax.fori_loop(0, NX, load, 0)

    order, order_next = order_a, order_b
    pops, pops_next = pops_a, pops_b
    for step in range(ITERS):
        left = 4 * (ITERS - 1 - step)
        last = step == ITERS - 1

        def chem_of(n, _, order=order, left=left, first=-3 if last else 0):
            x = (n + first) & 15
            up, down = (x + 1) & 15, (x - 1) & 15
            for r in tiles(left + 3):
                here = order[x, pl.ds(r, 8), :]
                beside = (order[up, pl.ds(r, 8), :] + order[down, pl.ds(r, 8), :]) + (
                    order[x, pl.ds(r + 1, 8), :] + order[x, pl.ds(r - 1, 8), :]
                )
                beside = beside + (next_lane(here) + prev_lane(here))
                chem[x, pl.ds(r, 8), :] = here * ((quadratic + 6.0 * stiffness) + quartic * (here * here)) - stiffness * beside
            return 0

        lax.fori_loop(0, 14 if last else 16, chem_of, 0)

        def collide_of(n, _, step=step, order=order, pops=pops, pops_next=pops_next, left=left, first=-2 if last else 0):
            x = (n + first) & 15
            up, down = (x + 1) & 15, (x - 1) & 15
            to = {0: x, 1: up, -1: down}
            for r in tiles(left + 2):
                at = pl.ds(r, 8)
                mu = chem[x, at, :]
                density = rho[x, at, :]
                inverse = 1.0 / density if step == 0 else inv[x, at, :]
                pull = (-0.5 * order[x, at, :]) * inverse
                kick = [
                    pull * (chem[up, at, :] - chem[down, at, :]),
                    pull * (chem[x, pl.ds(r + 1, 8), :] - chem[x, pl.ds(r - 1, 8), :]),
                    pull * (next_lane(mu) - prev_lane(mu)),
                ]
                old = None if step == 0 else (lambda i: pops[i, x, at, :])
                post = collide(density, [vel[d, x, at, :] for d in range(3)], kick, old)
                for i in range(19):
                    cx, cy, cz = DIRECTIONS[i]
                    value = post[i]
                    if cz:
                        value = prev_lane(value) if cz == 1 else next_lane(value)
                    pops_next[i, to[cx], pl.ds(r + cy, 8), :] = value
            return 0

        lax.fori_loop(0, 12 if last else 16, collide_of, 0)

        def flow_of(n, _, pops_next=pops_next, left=left, first=-1 if last else 0):
            x = (n + first) & 15
            for r in tiles(left + 1):
                at = pl.ds(r, 8)
                total, moms = moments([pops_next[i, x, at, :] for i in range(19)])
                inverse = 1.0 / total
                rho[x, at, :] = total
                inv[x, at, :] = inverse
                for d in range(3):
                    vel[d, x, at, :] = moms[d] * inverse
            return 0

        lax.fori_loop(0, 10 if last else 16, flow_of, 0)

        def order_of(x, _, order=order, order_next=order_next, left=left):
            up, down = (x + 1) & 15, (x - 1) & 15
            for r in tiles(left):
                at, north, south = pl.ds(r, 8), pl.ds(r + 1, 8), pl.ds(r - 1, 8)
                here = order[x, at, :]
                mu = chem[x, at, :]
                ux, uy, uz = (vel[d, x, at, :] for d in range(3))
                total = (ux + vel[0, up, at, :]) * (here + order[up, at, :]) - (ux + vel[0, down, at, :]) * (here + order[down, at, :])
                total = total + (uy + vel[1, x, north, :]) * (here + order[x, north, :])
                total = total - (uy + vel[1, x, south, :]) * (here + order[x, south, :])
                spread = (chem[up, at, :] + chem[down, at, :]) + (chem[x, north, :] + chem[x, south, :]) - 4.0 * mu
                face = (0.25 * (uz + next_lane(uz))) * (here + next_lane(here)) - mobility * (next_lane(mu) - mu)
                order_next[x, at, :] = here - ((0.25 * total - mobility * spread) + (face - prev_lane(face)))
            return 0

        lax.fori_loop(0, 8 if last else 16, order_of, 0)
        order, order_next = order_next, order
        pops, pops_next = pops_next, pops

    for target, base in ((mine_ref, core * 4), (send_ref, 4 - core * 4)):
        for x in range(4):
            for i in range(19):
                target[i, x] = pops[i, base + x, pl.ds(OWN, 16), :]
            target[19, x] = order[base + x, pl.ds(OWN, 16), :]


def vmem_call(kernel, outs, scratch=(), limit=None):
    space = pl.BlockSpec(memory_space=pltpu.VMEM)

    def call(core, *args):
        return pl.pallas_call(
            kernel,
            out_shape=[jax.ShapeDtypeStruct(s, F32) for s in outs],
            in_specs=[pl.BlockSpec(memory_space=pltpu.SMEM)] + [space] * len(args),
            out_specs=[space] * len(outs),
            scratch_shapes=[pltpu.VMEM(s, F32) for s in scratch],
            compiler_params=pltpu.CompilerParams(vmem_limit_bytes=limit or 24 << 20),
        )(core, *args)

    return call


def on_device(order_param, density, velocity):
    sizes = [lax.axis_size(a) for a in AXES]

    def send(value, to):
        pairs = []
        for x in range(sizes[0]):
            for y in range(sizes[1]):
                for z in range(sizes[2]):
                    tx, ty, tz = to(x, y, z)
                    there = (tx % sizes[0] * sizes[1] + ty % sizes[1]) * sizes[2] + tz % sizes[2]
                    pairs.append(((x * sizes[1] + y) * sizes[2] + z, there))
        return lax.ppermute(value, AXES, pairs)

    core = lax.rem(lax.axis_index("gx"), 2)
    core_arg = core.astype(jnp.int32).reshape(1)
    fields = jnp.concatenate([order_param[None], density[None], velocity])
    other = lax.ppermute(fields, "gx", [(i, i ^ 1) for i in range(sizes[0])])
    near, edge = vmem_call(gather_pair, [(5, 8, BY, LANES), (8, BY, LANES)])(core_arg, fields, other)
    far = lax.ppermute(near, "gx", [(i, i ^ 2) for i in range(sizes[0])])
    near_edge = send(edge, lambda x, y, z: (x ^ 1, y, z + 1 if x & 1 else z - 1))
    far_edge = send(edge, lambda x, y, z: (x ^ 3, y, z + 1 if x & 1 else z - 1))
    whole, last_rows, first_rows = vmem_call(merge_edges, [(5, NX, BY, LANES), (8, 24, LANES), (8, 24, LANES)])(
        core_arg, near, far, near_edge, far_edge
    )
    low = lax.ppermute(whole, "gy", [(i, (i + 1) % sizes[1]) for i in range(sizes[1])])
    high = lax.ppermute(whole, "gy", [(i, (i - 1) % sizes[1]) for i in range(sizes[1])])
    low2 = lax.ppermute(last_rows, "gy", [(i, (i + 2) % sizes[1]) for i in range(sizes[1])])
    high2 = lax.ppermute(first_rows, "gy", [(i, (i - 2) % sizes[1]) for i in range(sizes[1])])
    field = (NX, ROWS, LANES)
    mine, away = vmem_call(
        steps_kernel,
        [(20, 4, BY, LANES)] * 2,
        [(19,) + field, (19,) + field, field, field, field, field, field, (3,) + field],
        60 << 20,
    )(core_arg, whole, low, high, low2, high2)
    back = lax.ppermute(away, "gx", [(i, i ^ 1) for i in range(sizes[0])])
    half = lax.broadcasted_iota(jnp.int32, (1, 1, 1, LANES), 3) >= LANES // 2
    full = jnp.where(half == (core == 1), mine, back)
    return (full[19], full[:19])


def solution(mesh):
    return jax.shard_map(
        on_device,
        mesh=mesh,
        in_specs=(P("gx", "gy", "gz"), P("gx", "gy", "gz"), P(None, "gx", "gy", "gz")),
        out_specs=(P("gx", "gy", "gz"), P(None, "gx", "gy", "gz")),
        check_vma=False,
    )
```

```python
import jax
import jax.numpy as jnp
from jax import lax
from jax.experimental import pallas as pl
from jax.experimental.pallas import tpu as pltpu
from jax.sharding import PartitionSpec as P

ITERS = 5
DIRECTIONS = [
    (0, 0, 0),
    (1, 0, 0),
    (-1, 0, 0),
    (0, 1, 0),
    (0, -1, 0),
    (0, 0, 1),
    (0, 0, -1),
    (1, 1, 0),
    (-1, -1, 0),
    (1, -1, 0),
    (-1, 1, 0),
    (1, 0, 1),
    (-1, 0, -1),
    (1, 0, -1),
    (-1, 0, 1),
    (0, 1, 1),
    (0, -1, -1),
    (0, 1, -1),
    (0, -1, 1),
]
INDEX = {c: i for i, c in enumerate(DIRECTIONS)}
quadratic = -0.1
quartic = 0.1
stiffness = 0.02
mobility = 0.5

AXES = ("gx", "gy", "gz")
F32 = jnp.float32
NX = 16
BY = 16
LANES = 128
EDGE = 20
GAP = 24
ROWS = 80
OWN = 30


def tiles(radius):
    low = (OWN - radius) // 8 * 8
    high = -(-(OWN + BY + radius) // 8) * 8
    return list(range(low, high, 8))


def lane_masks(core, shape):
    lane = lax.broadcasted_iota(jnp.int32, shape, len(shape) - 1)
    low, high = lane < EDGE, lane >= LANES - EDGE
    first = core == 0
    send = (first & low) | (jnp.logical_not(first) & high)
    take = (first & high) | (jnp.logical_not(first) & low)
    return send, take


def gather_pair(core_ref, mine_ref, other_ref, both_ref, edge_ref):
    core = core_ref[0]
    lo, hi = core * 4, 4 - core * 4
    send, _ = lane_masks(core, (BY, LANES))
    for source, base in ((mine_ref, lo), (other_ref, hi)):
        for x in range(4):
            packed = None
            for f in range(5):
                value = source[f, x]
                both_ref[f, base + x] = value
                part = jnp.where(send, value, 0.0)
                part = pltpu.roll(part, GAP * f, 1) if f else part
                packed = part if packed is None else packed + part
            edge_ref[base + x] = packed


def merge_edges(core_ref, near_ref, far_ref, near_edge, far_edge, out_ref, up_ref, down_ref):
    _, take = lane_masks(core_ref[0], (BY, LANES))
    for x in range(NX):
        source, edges = (near_ref, near_edge) if x < 8 else (far_ref, far_edge)
        edge = edges[x % 8]
        row = (x % 2) * 12
        for f in range(5):
            moved = pltpu.roll(edge, LANES - GAP * f, 1) if f else edge
            value = jnp.where(take, moved, source[f, x % 8])
            out_ref[f, x] = value
            count = 4 if f == 0 else 2
            up_ref[x // 2, row : row + count, :] = value[BY - count :]
            down_ref[x // 2, row : row + count, :] = value[:count]
            row += count


def prev_lane(v):
    return pltpu.roll(v, 1, 1)


def next_lane(v):
    return pltpu.roll(v, LANES - 1, 1)


def collide(density, vel, kick, old):
    moved = [v + g for v, g in zip(vel, kick)]
    pairs = ((0, 1), (0, 2), (1, 2))
    if old is None:
        unit = density * (1.0 / 36.0)
        rest = unit
        drift = moved
        square = [m * m for m in moved]
        cross = [moved[d] * moved[e] for d, e in pairs]
    else:
        unit = density * (-4.0 / 36.0)
        rest = density * (-5.0 / 36.0)
        drift = [1.25 * v + g for v, g in zip(vel, kick)]
        square = [v * b + g * m for v, g, b, m in zip(vel, kick, drift, moved)]
        cross = [vel[d] * drift[e] + kick[d] * moved[e] for d, e in pairs]
    unit3 = unit * 3.0
    unit45 = unit * 4.5
    unit9 = unit * 9.0
    sq = [unit45 * v for v in square]
    cr = [unit9 * v for v in cross]
    dr = [unit3 * v for v in drift]
    base = rest - (1.0 / 3.0) * (sq[0] + sq[1] + sq[2])

    def settle(i, value):
        return value if old is None else value + old(i)

    post = {0: settle(0, 12.0 * base)}
    axis = [base + v for v in sq]
    for d in range(3):
        even = 2.0 * axis[d]
        odd = 2.0 * dr[d]
        c = [0, 0, 0]
        c[d] = 1
        i = INDEX[tuple(c)]
        post[i] = settle(i, even + odd)
        c[d] = -1
        i = INDEX[tuple(c)]
        post[i] = settle(i, even - odd)
    for k, (d, e) in enumerate(pairs):
        even = axis[d] + sq[e]
        for sign in (1, -1):
            part = even + cr[k] if sign == 1 else even - cr[k]
            odd = dr[d] + dr[e] if sign == 1 else dr[d] - dr[e]
            c = [0, 0, 0]
            c[d], c[e] = 1, sign
            i = INDEX[tuple(c)]
            post[i] = settle(i, part + odd)
            c[d], c[e] = -1, -sign
            i = INDEX[tuple(c)]
            post[i] = settle(i, part - odd)
    return post


def moments(f):
    both, diff = {}, {}
    for i in range(1, 19, 2):
        both[i] = f[i] + f[i + 1]
        diff[i] = f[i] - f[i + 1]
    rho = ((f[0] + both[1]) + (both[3] + both[5])) + (
        ((both[7] + both[9]) + (both[11] + both[13])) + (both[15] + both[17])
    )
    mx = (diff[1] + (diff[7] + diff[9])) + (diff[11] + diff[13])
    my = (diff[3] + (diff[7] - diff[9])) + (diff[15] + diff[17])
    mz = (diff[5] + (diff[11] - diff[13])) + (diff[15] - diff[17])
    return rho, (mx, my, mz)


def steps_kernel(core_ref, own, low, high, low2, high2, mine_ref, send_ref, pops_a, pops_b, order_a, order_b, chem, rho, inv, vel):
    core = core_ref[0]

    def load(pair, _):
        for half in range(2):
            x = 2 * pair + half
            for f, target in enumerate((order_a, rho, vel.at[0], vel.at[1], vel.at[2])):
                target[x, pl.ds(OWN - 16, 16), :] = low[f, x]
                target[x, pl.ds(OWN, 16), :] = own[f, x]
                target[x, pl.ds(OWN + 16, 16), :] = high[f, x]
                count, row = (4, 12 * half) if f == 0 else (2, 12 * half + 2 + 2 * f)
                target[x, pl.ds(OWN - 16 - count, count), :] = low2[pair, row : row + count, :]
                target[x, pl.ds(OWN + 32, count), :] = high2[pair, row : row + count, :]
        return 0

    lax.fori_loop(0, NX // 2, load, 0)

    order, order_next = order_a, order_b
    pops, pops_next = pops_a, pops_b
    for step in range(ITERS):
        left = 4 * (ITERS - 1 - step)
        last = step == ITERS - 1

        def chem_of(n, _, order=order, left=left, first=-3 if last else 0):
            x = (n + first) & 15
            up, down = (x + 1) & 15, (x - 1) & 15
            for r in tiles(left + 3):
                here = order[x, pl.ds(r, 8), :]
                beside = (order[up, pl.ds(r, 8), :] + order[down, pl.ds(r, 8), :]) + (
                    order[x, pl.ds(r + 1, 8), :] + order[x, pl.ds(r - 1, 8), :]
                )
                beside = beside + (next_lane(here) + prev_lane(here))
                chem[x, pl.ds(r, 8), :] = here * ((quadratic + 6.0 * stiffness) + quartic * (here * here)) - stiffness * beside
            return 0

        lax.fori_loop(0, 14 if last else 16, chem_of, 0, unroll=4)

        def collide_of(n, _, step=step, order=order, pops=pops, pops_next=pops_next, left=left, first=-2 if last else 0):
            x = (n + first) & 15
            up, down = (x + 1) & 15, (x - 1) & 15
            to = {0: x, 1: up, -1: down}
            for r in tiles(left + 2):
                at = pl.ds(r, 8)
                mu = chem[x, at, :]
                density = rho[x, at, :]
                inverse = 1.0 / density if step == 0 else inv[x, at, :]
                pull = ((-0.5 * (-4.0) ** max(step - 1, 0)) * order[x, at, :]) * inverse
                kick = [
                    pull * (chem[up, at, :] - chem[down, at, :]),
                    pull * (chem[x, pl.ds(r + 1, 8), :] - chem[x, pl.ds(r - 1, 8), :]),
                    pull * (next_lane(mu) - prev_lane(mu)),
                ]
                old = None if step == 0 else (lambda i: pops[i, x, at, :])
                post = collide(density, [vel[d, x, at, :] for d in range(3)], kick, old)
                for i in range(19):
                    cx, cy, cz = DIRECTIONS[i]
                    value = post[i]
                    if cz:
                        value = prev_lane(value) if cz == 1 else next_lane(value)
                    pops_next[i, to[cx], pl.ds(r + cy, 8), :] = value
            return 0

        lax.fori_loop(0, 12 if last else 16, collide_of, 0, unroll=2)

        def flow_of(n, _, pops_next=pops_next, left=left, first=-1 if last else 0):
            x = (n + first) & 15
            for r in tiles(left + 1):
                at = pl.ds(r, 8)
                total, moms = moments([pops_next[i, x, at, :] for i in range(19)])
                inverse = 1.0 / total
                rho[x, at, :] = total
                inv[x, at, :] = inverse
                for d in range(3):
                    vel[d, x, at, :] = moms[d] * inverse
            return 0

        lax.fori_loop(0, 10 if last else 16, flow_of, 0, unroll=2)

        def order_of(x, _, order=order, order_next=order_next, left=left):
            up, down = (x + 1) & 15, (x - 1) & 15
            for r in tiles(left):
                at, north, south = pl.ds(r, 8), pl.ds(r + 1, 8), pl.ds(r - 1, 8)
                here = order[x, at, :]
                mu = chem[x, at, :]
                ux, uy, uz = (vel[d, x, at, :] for d in range(3))
                total = (ux + vel[0, up, at, :]) * (here + order[up, at, :]) - (ux + vel[0, down, at, :]) * (here + order[down, at, :])
                total = total + (uy + vel[1, x, north, :]) * (here + order[x, north, :])
                total = total - (uy + vel[1, x, south, :]) * (here + order[x, south, :])
                spread = (chem[up, at, :] + chem[down, at, :]) + (chem[x, north, :] + chem[x, south, :]) - 4.0 * mu
                face = (0.25 * (uz + next_lane(uz))) * (here + next_lane(here)) - mobility * (next_lane(mu) - mu)
                order_next[x, at, :] = here - ((0.25 * total - mobility * spread) + (face - prev_lane(face)))
            return 0

        lax.fori_loop(0, 8 if last else 16, order_of, 0, unroll=4)
        order, order_next = order_next, order
        pops, pops_next = pops_next, pops

    for target, base in ((mine_ref, core * 4), (send_ref, 4 - core * 4)):
        for x in range(4):
            for i in range(19):
                target[i, x] = pops[i, base + x, pl.ds(OWN, 16), :] * (1.0 / 256.0)
            target[19, x] = order[base + x, pl.ds(OWN, 16), :]


def join_halves(core_ref, mine_ref, back_ref, order_ref, pops_ref):
    lane = lax.broadcasted_iota(jnp.int32, (4, BY, LANES), 2)
    first = core_ref[0] == 0
    keep = (first & (lane < LANES // 2)) | (jnp.logical_not(first) & (lane >= LANES // 2))
    for i in range(19):
        pops_ref[i] = jnp.where(keep, mine_ref[i], back_ref[i])
    order_ref[...] = jnp.where(keep, mine_ref[19], back_ref[19])


def vmem_call(kernel, outs, scratch=(), limit=None):
    space = pl.BlockSpec(memory_space=pltpu.VMEM)

    def call(core, *args):
        return pl.pallas_call(
            kernel,
            out_shape=[jax.ShapeDtypeStruct(s, F32) for s in outs],
            in_specs=[pl.BlockSpec(memory_space=pltpu.SMEM)] + [space] * len(args),
            out_specs=[space] * len(outs),
            scratch_shapes=[pltpu.VMEM(s, F32) for s in scratch],
            compiler_params=pltpu.CompilerParams(vmem_limit_bytes=limit or 24 << 20),
        )(core, *args)

    return call


def on_device(order_param, density, velocity):
    sizes = [lax.axis_size(a) for a in AXES]

    def send(value, to):
        pairs = []
        for x in range(sizes[0]):
            for y in range(sizes[1]):
                for z in range(sizes[2]):
                    tx, ty, tz = to(x, y, z)
                    there = (tx % sizes[0] * sizes[1] + ty % sizes[1]) * sizes[2] + tz % sizes[2]
                    pairs.append(((x * sizes[1] + y) * sizes[2] + z, there))
        return lax.ppermute(value, AXES, pairs)

    core = lax.rem(lax.axis_index("gx"), 2)
    core_arg = core.astype(jnp.int32).reshape(1)
    fields = jnp.concatenate([order_param[None], density[None], velocity])
    other = lax.ppermute(fields, "gx", [(i, i ^ 1) for i in range(sizes[0])])
    near, edge = vmem_call(gather_pair, [(5, 8, BY, LANES), (8, BY, LANES)])(core_arg, fields, other)
    far = lax.ppermute(near, "gx", [(i, i ^ 2) for i in range(sizes[0])])
    near_edge = send(edge, lambda x, y, z: (x ^ 1, y, z + 1 if x & 1 else z - 1))
    far_edge = send(edge, lambda x, y, z: (x ^ 3, y, z + 1 if x & 1 else z - 1))
    whole, last_rows, first_rows = vmem_call(merge_edges, [(5, NX, BY, LANES), (8, 24, LANES), (8, 24, LANES)])(
        core_arg, near, far, near_edge, far_edge
    )
    low = lax.ppermute(whole, "gy", [(i, (i + 1) % sizes[1]) for i in range(sizes[1])])
    high = lax.ppermute(whole, "gy", [(i, (i - 1) % sizes[1]) for i in range(sizes[1])])
    low2 = lax.ppermute(last_rows, "gy", [(i, (i + 2) % sizes[1]) for i in range(sizes[1])])
    high2 = lax.ppermute(first_rows, "gy", [(i, (i - 2) % sizes[1]) for i in range(sizes[1])])
    field = (NX, ROWS, LANES)
    mine, away = vmem_call(
        steps_kernel,
        [(20, 4, BY, LANES)] * 2,
        [(19,) + field, (19,) + field, field, field, field, field, field, (3,) + field],
        60 << 20,
    )(core_arg, whole, low, high, low2, high2)
    back = lax.ppermute(away, "gx", [(i, i ^ 1) for i in range(sizes[0])])
    return tuple(vmem_call(join_halves, [(4, BY, LANES), (19, 4, BY, LANES)])(core_arg, mine, back))


def solution(mesh):
    return jax.shard_map(
        on_device,
        mesh=mesh,
        in_specs=(P("gx", "gy", "gz"), P("gx", "gy", "gz"), P(None, "gx", "gy", "gz")),
        out_specs=(P("gx", "gy", "gz"), P(None, "gx", "gy", "gz")),
        check_vma=False,
    )
```

```python
import jax
import jax.numpy as jnp
from jax import lax
from jax.experimental import pallas as pl
from jax.experimental.pallas import tpu as pltpu
from jax.sharding import PartitionSpec as P

ITERS = 5
DIRECTIONS = [
    (0, 0, 0),
    (1, 0, 0),
    (-1, 0, 0),
    (0, 1, 0),
    (0, -1, 0),
    (0, 0, 1),
    (0, 0, -1),
    (1, 1, 0),
    (-1, -1, 0),
    (1, -1, 0),
    (-1, 1, 0),
    (1, 0, 1),
    (-1, 0, -1),
    (1, 0, -1),
    (-1, 0, 1),
    (0, 1, 1),
    (0, -1, -1),
    (0, 1, -1),
    (0, -1, 1),
]
INDEX = {c: i for i, c in enumerate(DIRECTIONS)}
quadratic = -0.1
quartic = 0.1
stiffness = 0.02
mobility = 0.5

AXES = ("gx", "gy", "gz")
F32 = jnp.float32
NX = 16
BY = 16
LANES = 128
EDGE = 20
PART = 26
GAP = 24
ROWS = 80
OWN = 30


def tiles(radius):
    return [OWN - radius + 8 * k for k in range(-(-(BY + 2 * radius) // 8))]


def lane_masks(core, shape):
    lane = lax.broadcasted_iota(jnp.int32, shape, len(shape) - 1)
    low, high = lane < EDGE, lane >= LANES - EDGE
    first = core == 0
    send = (first & low) | (jnp.logical_not(first) & high)
    take = (first & high) | (jnp.logical_not(first) & low)
    return send, take


def gather_pair(core_ref, mine_ref, other_ref, both_ref, edge_ref):
    core = core_ref[0]
    lo, hi = core * 4, 4 - core * 4
    send, _ = lane_masks(core, (BY, LANES))
    for source, base in ((mine_ref, lo), (other_ref, hi)):
        for x in range(4):
            packed = None
            for f in range(5):
                value = source[f, x]
                both_ref[f, base + x] = value
                part = jnp.where(send, value, 0.0)
                part = pltpu.roll(part, GAP * f, 1) if f else part
                packed = part if packed is None else packed + part
            edge_ref[base + x] = packed


def spare_lanes(core, shape):
    lane = lax.broadcasted_iota(jnp.int32, shape, len(shape) - 1)
    start = jnp.where(core == 0, 82, 18)
    return (lane >= start) & (lane < start + PART), lane, start


def merge_edges(core_ref, near_ref, far_ref, other_ref, near_edge, far_edge, pack_ref, up_ref, down_ref):
    core = core_ref[0]
    lo, hi = core * 4, 4 - core * 4
    _, take = lane_masks(core, (BY, LANES))
    spare, _, _ = spare_lanes(core, (BY, LANES))
    for n in range(NX):
        if n < 8:
            source, k, x, edge = near_ref, n, n, near_edge[n]
        else:
            source, k, base = (far_ref, n - 8, lo) if n < 12 else (other_ref, n - 12, hi)
            x = base + 8 + n % 4
            edge = far_edge[x - 8]
        pair, row = (x // 2, (x % 2) * 12) if n < 8 else (lax.div(base, 2) + 4 + n % 4 // 2, (n % 2) * 12)
        order = None
        for f in range(5):
            moved = pltpu.roll(edge, LANES - GAP * f, 1) if f else edge
            value = jnp.where(take, moved, source[f, k])
            if f == 0:
                order = value
            else:
                pack_ref[f - 1, x] = jnp.where(spare, pltpu.roll(order, LANES - PART * f, 1), value)
            count = 4 if f == 0 else 2
            up_ref[pair, row : row + count, :] = value[BY - count :]
            down_ref[pair, row : row + count, :] = value[:count]
            row += count


def prev_lane(v):
    return pltpu.roll(v, 1, 1)


def next_lane(v):
    return pltpu.roll(v, LANES - 1, 1)


def collide(density, vel, kick, old):
    moved = [v + g for v, g in zip(vel, kick)]
    pairs = ((0, 1), (0, 2), (1, 2))
    if old is None:
        unit = density * (1.0 / 36.0)
        rest = unit
        drift = moved
        square = [m * m for m in moved]
        cross = [moved[d] * moved[e] for d, e in pairs]
    else:
        unit = density * (-4.0 / 36.0)
        rest = density * (-5.0 / 36.0)
        drift = [1.25 * v + g for v, g in zip(vel, kick)]
        square = [v * b + g * m for v, g, b, m in zip(vel, kick, drift, moved)]
        cross = [vel[d] * drift[e] + kick[d] * moved[e] for d, e in pairs]
    unit3 = unit * 3.0
    unit45 = unit * 4.5
    unit9 = unit * 9.0
    sq = [unit45 * v for v in square]
    cr = [unit9 * v for v in cross]
    dr = [unit3 * v for v in drift]
    base = rest - (1.0 / 3.0) * (sq[0] + sq[1] + sq[2])

    def settle(i, value):
        return value if old is None else value + old(i)

    post = {0: settle(0, 12.0 * base)}
    axis = [base + v for v in sq]
    for d in range(3):
        even = 2.0 * axis[d]
        odd = 2.0 * dr[d]
        c = [0, 0, 0]
        c[d] = 1
        i = INDEX[tuple(c)]
        post[i] = settle(i, even + odd)
        c[d] = -1
        i = INDEX[tuple(c)]
        post[i] = settle(i, even - odd)
    for k, (d, e) in enumerate(pairs):
        even = axis[d] + sq[e]
        for sign in (1, -1):
            part = even + cr[k] if sign == 1 else even - cr[k]
            odd = dr[d] + dr[e] if sign == 1 else dr[d] - dr[e]
            c = [0, 0, 0]
            c[d], c[e] = 1, sign
            i = INDEX[tuple(c)]
            post[i] = settle(i, part + odd)
            c[d], c[e] = -1, -sign
            i = INDEX[tuple(c)]
            post[i] = settle(i, part - odd)
    return post


def moments(f):
    both, diff = {}, {}
    for i in range(1, 19, 2):
        both[i] = f[i] + f[i + 1]
        diff[i] = f[i] - f[i + 1]
    rho = ((f[0] + both[1]) + (both[3] + both[5])) + (
        ((both[7] + both[9]) + (both[11] + both[13])) + (both[15] + both[17])
    )
    mx = (diff[1] + (diff[7] + diff[9])) + (diff[11] + diff[13])
    my = (diff[3] + (diff[7] - diff[9])) + (diff[15] + diff[17])
    mz = (diff[5] + (diff[11] - diff[13])) + (diff[15] - diff[17])
    return rho, (mx, my, mz)


def steps_kernel(core_ref, own, low, high, low2, high2, mine_ref, send_ref, pops_a, pops_b, order_a, order_b, chem, rho, inv, vel):
    core = core_ref[0]

    targets = (order_a, rho, vel.at[0], vel.at[1], vel.at[2])
    _, lane, start = spare_lanes(core, (BY, LANES))
    source_lane = lax.rem(lane - start + 2 * LANES - PART, LANES)

    def load(pair, _):
        for half in range(2):
            x = 2 * pair + half
            for source, row in ((low, OWN - 16), (own, OWN), (high, OWN + 16)):
                order = None
                for f in range(1, 5):
                    value = source[f - 1, x]
                    targets[f][x, pl.ds(row, 16), :] = value
                    moved = pltpu.roll(value, PART * f, 1)
                    order = moved if order is None else jnp.where(source_lane >= PART * (f - 1), moved, order)
                order_a[x, pl.ds(row, 16), :] = order
            for f, target in enumerate(targets):
                count, row = (4, 12 * half) if f == 0 else (2, 12 * half + 2 + 2 * f)
                target[x, pl.ds(OWN - 16 - count, count), :] = low2[pair, row : row + count, :]
                target[x, pl.ds(OWN + 32, count), :] = high2[pair, row : row + count, :]
        return 0

    lax.fori_loop(0, NX // 2, load, 0)

    order, order_next = order_a, order_b
    pops, pops_next = pops_a, pops_b
    for step in range(ITERS):
        left = 4 * (ITERS - 1 - step)
        last = step == ITERS - 1

        def chem_of(n, _, order=order, left=left, first=-3 if last else 0):
            x = (n + first) & 15
            up, down = (x + 1) & 15, (x - 1) & 15
            for r in tiles(left + 3):
                here = order[x, pl.ds(r, 8), :]
                beside = (order[up, pl.ds(r, 8), :] + order[down, pl.ds(r, 8), :]) + (
                    order[x, pl.ds(r + 1, 8), :] + order[x, pl.ds(r - 1, 8), :]
                )
                beside = beside + (next_lane(here) + prev_lane(here))
                chem[x, pl.ds(r, 8), :] = here * ((quadratic + 6.0 * stiffness) + quartic * (here * here)) - stiffness * beside
            return 0

        lax.fori_loop(0, 14 if last else 16, chem_of, 0, unroll=4)

        def collide_of(n, _, step=step, order=order, pops=pops, pops_next=pops_next, left=left, first=-2 if last else 0):
            x = (n + first) & 15
            up, down = (x + 1) & 15, (x - 1) & 15
            to = {0: x, 1: up, -1: down}
            for r in tiles(left + 2):
                at = pl.ds(r, 8)
                mu = chem[x, at, :]
                density = rho[x, at, :]
                inverse = 1.0 / density if step == 0 else inv[x, at, :]
                pull = ((-0.5 * (-4.0) ** max(step - 1, 0)) * order[x, at, :]) * inverse
                kick = [
                    pull * (chem[up, at, :] - chem[down, at, :]),
                    pull * (chem[x, pl.ds(r + 1, 8), :] - chem[x, pl.ds(r - 1, 8), :]),
                    pull * (next_lane(mu) - prev_lane(mu)),
                ]
                old = None if step == 0 else (lambda i: pops[i, x, at, :])
                post = collide(density, [vel[d, x, at, :] for d in range(3)], kick, old)
                for i in range(19):
                    cx, cy, cz = DIRECTIONS[i]
                    value = post[i]
                    if cz:
                        value = prev_lane(value) if cz == 1 else next_lane(value)
                    pops_next[i, to[cx], pl.ds(r + cy, 8), :] = value
            return 0

        lax.fori_loop(0, 12 if last else 16, collide_of, 0, unroll=2)

        def flow_of(n, _, pops_next=pops_next, left=left, first=-1 if last else 0):
            x = (n + first) & 15
            for r in tiles(left + 1):
                at = pl.ds(r, 8)
                total, moms = moments([pops_next[i, x, at, :] for i in range(19)])
                inverse = 1.0 / total
                rho[x, at, :] = total
                inv[x, at, :] = inverse
                for d in range(3):
                    vel[d, x, at, :] = moms[d] * inverse
            return 0

        lax.fori_loop(0, 10 if last else 16, flow_of, 0, unroll=2)

        def order_of(x, _, order=order, order_next=order_next, left=left):
            up, down = (x + 1) & 15, (x - 1) & 15
            for r in tiles(left):
                at, north, south = pl.ds(r, 8), pl.ds(r + 1, 8), pl.ds(r - 1, 8)
                here = order[x, at, :]
                mu = chem[x, at, :]
                ux, uy, uz = (vel[d, x, at, :] for d in range(3))
                total = (ux + vel[0, up, at, :]) * (here + order[up, at, :]) - (ux + vel[0, down, at, :]) * (here + order[down, at, :])
                total = total + (uy + vel[1, x, north, :]) * (here + order[x, north, :])
                total = total - (uy + vel[1, x, south, :]) * (here + order[x, south, :])
                spread = (chem[up, at, :] + chem[down, at, :]) + (chem[x, north, :] + chem[x, south, :]) - 4.0 * mu
                face = (0.25 * (uz + next_lane(uz))) * (here + next_lane(here)) - mobility * (next_lane(mu) - mu)
                order_next[x, at, :] = here - ((0.25 * total - mobility * spread) + (face - prev_lane(face)))
            return 0

        lax.fori_loop(0, 8 if last else 16, order_of, 0, unroll=4)
        order, order_next = order_next, order
        pops, pops_next = pops_next, pops

    keep = kept_lanes(core, (BY, LANES))
    for x in range(4):
        for i in range(20):
            source, scale = (order, None) if i == 19 else (pops.at[i], 1.0 / 256.0)
            here = source[core * 4 + x, pl.ds(OWN, 16), :]
            mine_ref[i, x] = here if scale is None else here * scale
            there = source[4 - core * 4 + x, pl.ds(OWN, 16), :]
            there = there if scale is None else there * scale
            if i % 2 == 0:
                first = there
            else:
                send_ref[i // 2, x] = jnp.where(keep, first, pltpu.roll(there, LANES // 2, 1))


def kept_lanes(core, shape):
    lane = lax.broadcasted_iota(jnp.int32, shape, len(shape) - 1)
    first = core == 0
    return (first & (lane < LANES // 2)) | (jnp.logical_not(first) & (lane >= LANES // 2))


def join_halves(core_ref, mine_ref, back_ref, order_ref, pops_ref):
    keep = kept_lanes(core_ref[0], (BY, LANES))
    for x in range(4):
        for i in range(20):
            back = back_ref[i // 2, x]
            value = jnp.where(keep, mine_ref[i, x], pltpu.roll(back, LANES // 2, 1) if i % 2 else back)
            if i == 19:
                order_ref[x] = value
            else:
                pops_ref[i, x] = value


def vmem_call(kernel, outs, scratch=(), limit=None):
    space = pl.BlockSpec(memory_space=pltpu.VMEM)

    def call(core, *args):
        return pl.pallas_call(
            kernel,
            out_shape=[jax.ShapeDtypeStruct(s, F32) for s in outs],
            in_specs=[pl.BlockSpec(memory_space=pltpu.SMEM)] + [space] * len(args),
            out_specs=[space] * len(outs),
            scratch_shapes=[pltpu.VMEM(s, F32) for s in scratch],
            compiler_params=pltpu.CompilerParams(vmem_limit_bytes=limit or 24 << 20),
        )(core, *args)

    return call


def on_device(order_param, density, velocity):
    sizes = [lax.axis_size(a) for a in AXES]

    def send(value, to):
        pairs = []
        for x in range(sizes[0]):
            for y in range(sizes[1]):
                for z in range(sizes[2]):
                    tx, ty, tz = to(x, y, z)
                    there = (tx % sizes[0] * sizes[1] + ty % sizes[1]) * sizes[2] + tz % sizes[2]
                    pairs.append(((x * sizes[1] + y) * sizes[2] + z, there))
        return lax.ppermute(value, AXES, pairs)

    core = lax.rem(lax.axis_index("gx"), 2)
    core_arg = core.astype(jnp.int32).reshape(1)
    fields = jnp.concatenate([order_param[None], density[None], velocity])
    def along(value, axis, to):
        return lax.ppermute(value, axis, [(i, to(i) % lax.axis_size(axis)) for i in range(lax.axis_size(axis))])

    def swap(i):
        return i ^ 1

    other = along(fields, "gx", swap)
    far = along(fields, "gx", lambda i: i ^ 2)
    near, edge = vmem_call(gather_pair, [(5, 8, BY, LANES), (8, BY, LANES)])(core_arg, fields, other)
    near_edge = send(edge, lambda x, y, z: (x ^ 1, y, z + 1 if x & 1 else z - 1))
    far_edge = send(edge, lambda x, y, z: (x ^ 3, y, z + 1 if x & 1 else z - 1))
    far_again, near_edge, far_edge = lax.optimization_barrier((far, near_edge, far_edge))
    other_far = along(far_again, "gx", swap)
    pack, last_rows, first_rows = vmem_call(merge_edges, [(4, NX, BY, LANES), (8, 24, LANES), (8, 24, LANES)])(
        core_arg, near, far_again, other_far, near_edge, far_edge
    )
    low = along(pack, "gy", lambda i: i + 1)
    high = along(pack, "gy", lambda i: i - 1)
    low2 = along(last_rows, "gy", lambda i: i + 2)
    high2 = along(first_rows, "gy", lambda i: i - 2)
    field = (NX, ROWS, LANES)
    mine, away = vmem_call(
        steps_kernel,
        [(20, 4, BY, LANES), (10, 4, BY, LANES)],
        [(19,) + field, (19,) + field, field, field, field, field, field, (3,) + field],
        60 << 20,
    )(core_arg, pack, low, high, low2, high2)
    back = along(away, "gx", swap)
    return tuple(vmem_call(join_halves, [(4, BY, LANES), (19, 4, BY, LANES)])(core_arg, mine, back))


def solution(mesh):
    return jax.shard_map(
        on_device,
        mesh=mesh,
        in_specs=(P("gx", "gy", "gz"), P("gx", "gy", "gz"), P(None, "gx", "gy", "gz")),
        out_specs=(P("gx", "gy", "gz"), P(None, "gx", "gy", "gz")),
        check_vma=False,
    )
```

```python
import jax
import jax.numpy as jnp
from jax import lax
from jax.experimental import pallas as pl
from jax.experimental.pallas import tpu as pltpu
from jax.sharding import PartitionSpec as P

ITERS = 5
DIRECTIONS = [
    (0, 0, 0),
    (1, 0, 0),
    (-1, 0, 0),
    (0, 1, 0),
    (0, -1, 0),
    (0, 0, 1),
    (0, 0, -1),
    (1, 1, 0),
    (-1, -1, 0),
    (1, -1, 0),
    (-1, 1, 0),
    (1, 0, 1),
    (-1, 0, -1),
    (1, 0, -1),
    (-1, 0, 1),
    (0, 1, 1),
    (0, -1, -1),
    (0, 1, -1),
    (0, -1, 1),
]
INDEX = {c: i for i, c in enumerate(DIRECTIONS)}
quadratic = -0.1
quartic = 0.1
stiffness = 0.02
mobility = 0.5

AXES = ("gx", "gy", "gz")
F32 = jnp.float32
NX = 16
BY = 16
LANES = 128
EDGE = 20
PART = 26
GAP = 24
ROWS = 72
OWN = 30


def tiles(radius):
    return [OWN - radius + 8 * k for k in range(-(-(BY + 2 * radius) // 8))]


def lane_masks(core, shape):
    lane = lax.broadcasted_iota(jnp.int32, shape, len(shape) - 1)
    low, high = lane < EDGE, lane >= LANES - EDGE
    first = core == 0
    send = (first & low) | (jnp.logical_not(first) & high)
    take = (first & high) | (jnp.logical_not(first) & low)
    return send, take


def gather_pair(core_ref, mine_ref, other_ref, both_ref, edge_ref):
    core = core_ref[0]
    lo, hi = core * 4, 4 - core * 4
    send, _ = lane_masks(core, (BY, LANES))
    for source, base in ((mine_ref, lo), (other_ref, hi)):
        for x in range(4):
            packed = None
            for f in range(5):
                value = source[f, x]
                both_ref[f, base + x] = value
                part = jnp.where(send, value, 0.0)
                part = pltpu.roll(part, GAP * f, 1) if f else part
                packed = part if packed is None else packed + part
            edge_ref[base + x] = packed


def spare_lanes(core, shape):
    lane = lax.broadcasted_iota(jnp.int32, shape, len(shape) - 1)
    start = jnp.where(core == 0, 82, 18)
    return (lane >= start) & (lane < start + PART), lane, start


def merge_edges(core_ref, near_ref, far_ref, other_ref, near_edge, far_edge, pack_ref, up_ref, down_ref):
    core = core_ref[0]
    lo, hi = core * 4, 4 - core * 4
    _, take = lane_masks(core, (BY, LANES))
    spare, _, _ = spare_lanes(core, (BY, LANES))
    for n in range(NX):
        if n < 8:
            source, k, x, edge = near_ref, n, n, near_edge[n]
        else:
            source, k, base = (far_ref, n - 8, lo) if n < 12 else (other_ref, n - 12, hi)
            x = base + 8 + n % 4
            edge = far_edge[x - 8]
        pair, row = (x // 2, (x % 2) * 12) if n < 8 else (lax.div(base, 2) + 4 + n % 4 // 2, (n % 2) * 12)
        order = None
        for f in range(5):
            moved = pltpu.roll(edge, LANES - GAP * f, 1) if f else edge
            value = jnp.where(take, moved, source[f, k])
            if f == 0:
                order = value
            else:
                pack_ref[f - 1, x] = jnp.where(spare, pltpu.roll(order, LANES - PART * f, 1), value)
            count = 4 if f == 0 else 2
            up_ref[pair, row : row + count, :] = value[BY - count :]
            down_ref[pair, row : row + count, :] = value[:count]
            row += count


def prev_lane(v):
    return pltpu.roll(v, 1, 1)


def next_lane(v):
    return pltpu.roll(v, LANES - 1, 1)


def collide(density, vel, kick, old):
    moved = [v + g for v, g in zip(vel, kick)]
    pairs = ((0, 1), (0, 2), (1, 2))
    if old is None:
        unit = density * (1.0 / 36.0)
        rest = unit
        drift = moved
        square = [m * m for m in moved]
        cross = [moved[d] * moved[e] for d, e in pairs]
    else:
        unit = density * (-4.0 / 36.0)
        rest = density * (-5.0 / 36.0)
        drift = [1.25 * v + g for v, g in zip(vel, kick)]
        square = [v * b + g * m for v, g, b, m in zip(vel, kick, drift, moved)]
        cross = [vel[d] * drift[e] + kick[d] * moved[e] for d, e in pairs]
    unit3 = unit * 3.0
    unit45 = unit * 4.5
    unit9 = unit * 9.0
    sq = [unit45 * v for v in square]
    cr = [unit9 * v for v in cross]
    dr = [unit3 * v for v in drift]
    base = rest - (1.0 / 3.0) * (sq[0] + sq[1] + sq[2])

    def settle(i, value):
        return value if old is None else value + old(i)

    post = {0: settle(0, 12.0 * base)}
    axis = [base + v for v in sq]
    for d in range(3):
        even = 2.0 * axis[d]
        odd = 2.0 * dr[d]
        c = [0, 0, 0]
        c[d] = 1
        i = INDEX[tuple(c)]
        post[i] = settle(i, even + odd)
        c[d] = -1
        i = INDEX[tuple(c)]
        post[i] = settle(i, even - odd)
    for k, (d, e) in enumerate(pairs):
        even = axis[d] + sq[e]
        for sign in (1, -1):
            part = even + cr[k] if sign == 1 else even - cr[k]
            odd = dr[d] + dr[e] if sign == 1 else dr[d] - dr[e]
            c = [0, 0, 0]
            c[d], c[e] = 1, sign
            i = INDEX[tuple(c)]
            post[i] = settle(i, part + odd)
            c[d], c[e] = -1, -sign
            i = INDEX[tuple(c)]
            post[i] = settle(i, part - odd)
    return post


def moments(f):
    both, diff = {}, {}
    for i in range(1, 19, 2):
        both[i] = f[i] + f[i + 1]
        diff[i] = f[i] - f[i + 1]
    rho = ((f[0] + both[1]) + (both[3] + both[5])) + (
        ((both[7] + both[9]) + (both[11] + both[13])) + (both[15] + both[17])
    )
    mx = (diff[1] + (diff[7] + diff[9])) + (diff[11] + diff[13])
    my = (diff[3] + (diff[7] - diff[9])) + (diff[15] + diff[17])
    mz = (diff[5] + (diff[11] - diff[13])) + (diff[15] - diff[17])
    return rho, (mx, my, mz)


class Passes:
    def __init__(self, pops, order, chem, rho, inv, vel):
        self.pops, self.orders, self.chems, self.rho, self.inv, self.vel = pops, order, chem, rho, inv, vel

    def run(self, first, count, names, offset=None, unroll=1):
        behind = {"collide": 0, "flow": -3, "order": -6, "chem": 3}

        def body(n, _):
            for name, step in names:
                shift = behind[name] - 12 * step if offset is None else offset
                x = (n + shift) & (NX - 1)
                getattr(self, name)(step, x, (x + 1) & (NX - 1), (x - 1) & (NX - 1))
            return 0

        lax.fori_loop(first, first + count, body, 0, unroll=unroll)

    def left(self, step):
        return 4 * (ITERS - 1 - step)

    def chem(self, step, x, up, down):
        order, chem = self.orders[step % 2], self.chems[step % 2]
        for r in tiles(self.left(step) + 3):
            here = order[x, pl.ds(r, 8), :]
            beside = (order[up, pl.ds(r, 8), :] + order[down, pl.ds(r, 8), :]) + (
                order[x, pl.ds(r + 1, 8), :] + order[x, pl.ds(r - 1, 8), :]
            )
            beside = beside + (next_lane(here) + prev_lane(here))
            chem[x, pl.ds(r, 8), :] = here * ((quadratic + 6.0 * stiffness) + quartic * (here * here)) - stiffness * beside

    def collide(self, step, x, up, down):
        order, chem = self.orders[step % 2], self.chems[step % 2]
        was = (step - 1) % 2
        rho, inv, vel, old, new = self.rho[was], self.inv[was], self.vel[was], self.pops[was], self.pops[1 - was]
        to = {0: x, 1: up, -1: down}
        for r in tiles(self.left(step) + 2):
            at = pl.ds(r, 8)
            mu = chem[x, at, :]
            density = rho[x, at, :]
            inverse = 1.0 / density if step == 0 else inv[x, at, :]
            pull = ((-0.5 * (-4.0) ** max(step - 1, 0)) * order[x, at, :]) * inverse
            kick = [
                pull * (chem[up, at, :] - chem[down, at, :]),
                pull * (chem[x, pl.ds(r + 1, 8), :] - chem[x, pl.ds(r - 1, 8), :]),
                pull * (next_lane(mu) - prev_lane(mu)),
            ]
            before = None if step == 0 else (lambda i: old[i, x, at, :])
            post = collide(density, [vel[d, x, at, :] for d in range(3)], kick, before)
            for i in range(19):
                cx, cy, cz = DIRECTIONS[i]
                value = post[i]
                if cz:
                    value = prev_lane(value) if cz == 1 else next_lane(value)
                new[i, to[cx], pl.ds(r + cy, 8), :] = value

    def flow(self, step, x, up, down):
        now = step % 2
        for r in tiles(self.left(step) + 1):
            at = pl.ds(r, 8)
            total, moms = moments([self.pops[now][i, x, at, :] for i in range(19)])
            inverse = 1.0 / total
            self.rho[now][x, at, :] = total
            self.inv[now][x, at, :] = inverse
            for d in range(3):
                self.vel[now][d, x, at, :] = moms[d] * inverse

    def order(self, step, x, up, down):
        now = step % 2
        order, chem, vel = self.orders[now], self.chems[now], self.vel[now]
        for r in tiles(self.left(step)):
            at, north, south = pl.ds(r, 8), pl.ds(r + 1, 8), pl.ds(r - 1, 8)
            here = order[x, at, :]
            mu = chem[x, at, :]
            ux, uy, uz = (vel[d, x, at, :] for d in range(3))
            total = (ux + vel[0, up, at, :]) * (here + order[up, at, :])
            total = total - (ux + vel[0, down, at, :]) * (here + order[down, at, :])
            total = total + (uy + vel[1, x, north, :]) * (here + order[x, north, :])
            total = total - (uy + vel[1, x, south, :]) * (here + order[x, south, :])
            spread = (chem[up, at, :] + chem[down, at, :]) + (chem[x, north, :] + chem[x, south, :]) - 4.0 * mu
            face = (0.25 * (uz + next_lane(uz))) * (here + next_lane(here)) - mobility * (next_lane(mu) - mu)
            self.orders[1 - now][x, at, :] = here - ((0.25 * total - mobility * spread) + (face - prev_lane(face)))


def steps_kernel(core_ref, own, low, high, low2, high2, mine_ref, send_ref, pops_a, pops_b, order_a, order_b, chem_a, chem_b, rho_a, rho_b, inv_a, inv_b, vel_a, vel_b):
    core = core_ref[0]

    targets = (order_a, rho_b, vel_b.at[0], vel_b.at[1], vel_b.at[2])
    _, lane, start = spare_lanes(core, (BY, LANES))
    source_lane = lax.rem(lane - start + 2 * LANES - PART, LANES)

    def load(pair, _):
        for half in range(2):
            x = 2 * pair + half
            for source, row in ((low, OWN - 16), (own, OWN), (high, OWN + 16)):
                order = None
                for f in range(1, 5):
                    value = source[f - 1, x]
                    targets[f][x, pl.ds(row, 16), :] = value
                    moved = pltpu.roll(value, PART * f, 1)
                    order = moved if order is None else jnp.where(source_lane >= PART * (f - 1), moved, order)
                order_a[x, pl.ds(row, 16), :] = order
            for f, target in enumerate(targets):
                count, row = (4, 12 * half) if f == 0 else (2, 12 * half + 2 + 2 * f)
                target[x, pl.ds(OWN - 16 - count, count), :] = low2[pair, row : row + count, :]
                target[x, pl.ds(OWN + 32, count), :] = high2[pair, row : row + count, :]
        return 0

    lax.fori_loop(0, NX // 2, load, 0)

    passes = Passes((pops_a, pops_b), (order_a, order_b), (chem_a, chem_b), (rho_a, rho_b), (inv_a, inv_b), (vel_a, vel_b))
    run = passes.run
    run(0, NX, [("chem", 0)], offset=0, unroll=4)
    for step in range(ITERS - 1):
        start = 16 * step
        early = step > 0
        run(start, 4, [("collide", step)] + [("chem", step), ("order", step - 1), ("flow", step - 1)] * early)
        run(start + 4, 4, [("flow", step), ("collide", step)] + [("chem", step), ("order", step - 1)] * early)
        run(start + 8, 4, [("order", step), ("flow", step), ("collide", step)] + [("chem", step)] * early)
        run(start + 12, 4, [("chem", step + 1), ("order", step), ("flow", step), ("collide", step)])
    step = ITERS - 1
    start = 16 * step
    run(start, 4, [("collide", step), ("chem", step), ("order", step - 1), ("flow", step - 1)])
    run(start + 4, 4, [("flow", step), ("collide", step), ("chem", step), ("order", step - 1)])
    run(start + 8, 2, [("flow", step), ("collide", step), ("chem", step)])
    run(start + 10, 2, [("chem", step)], unroll=2)
    run(14, 2, [("collide", step)], offset=0, unroll=2)
    run(7, 2, [("flow", step)], offset=0, unroll=2)
    run(15, 2, [("flow", step)], offset=0, unroll=2)
    run(0, 8, [("order", step)], offset=0, unroll=4)
    pops = (pops_a, pops_b)[step % 2]
    order = (order_a, order_b)[ITERS % 2]

    keep = kept_lanes(core, (BY, LANES))
    for x in range(4):
        for i in range(20):
            source, scale = (order, None) if i == 19 else (pops.at[i], 1.0 / 256.0)
            here = source[core * 4 + x, pl.ds(OWN, 16), :]
            mine_ref[i, x] = here if scale is None else here * scale
            there = source[4 - core * 4 + x, pl.ds(OWN, 16), :]
            there = there if scale is None else there * scale
            if i % 2 == 0:
                first = there
            else:
                send_ref[i // 2, x] = jnp.where(keep, first, pltpu.roll(there, LANES // 2, 1))


def kept_lanes(core, shape):
    lane = lax.broadcasted_iota(jnp.int32, shape, len(shape) - 1)
    first = core == 0
    return (first & (lane < LANES // 2)) | (jnp.logical_not(first) & (lane >= LANES // 2))


def join_halves(core_ref, mine_ref, back_ref, order_ref, pops_ref):
    keep = kept_lanes(core_ref[0], (BY, LANES))
    for x in range(4):
        for i in range(20):
            back = back_ref[i // 2, x]
            value = jnp.where(keep, mine_ref[i, x], pltpu.roll(back, LANES // 2, 1) if i % 2 else back)
            if i == 19:
                order_ref[x] = value
            else:
                pops_ref[i, x] = value


def vmem_call(kernel, outs, scratch=(), limit=None):
    space = pl.BlockSpec(memory_space=pltpu.VMEM)

    def call(core, *args):
        return pl.pallas_call(
            kernel,
            out_shape=[jax.ShapeDtypeStruct(s, F32) for s in outs],
            in_specs=[pl.BlockSpec(memory_space=pltpu.SMEM)] + [space] * len(args),
            out_specs=[space] * len(outs),
            scratch_shapes=[pltpu.VMEM(s, F32) for s in scratch],
            compiler_params=pltpu.CompilerParams(vmem_limit_bytes=limit or 24 << 20),
        )(core, *args)

    return call


def make_steps():
    field = (NX, ROWS, LANES)
    return vmem_call(
        steps_kernel,
        [(20, 4, BY, LANES), (10, 4, BY, LANES)],
        [(19,) + field] * 2 + [field] * 8 + [(3,) + field] * 2,
        40 << 20,
    )


def on_device(order_param, density, velocity):
    sizes = [lax.axis_size(a) for a in AXES]

    def send(value, to):
        pairs = []
        for x in range(sizes[0]):
            for y in range(sizes[1]):
                for z in range(sizes[2]):
                    tx, ty, tz = to(x, y, z)
                    there = (tx % sizes[0] * sizes[1] + ty % sizes[1]) * sizes[2] + tz % sizes[2]
                    pairs.append(((x * sizes[1] + y) * sizes[2] + z, there))
        return lax.ppermute(value, AXES, pairs)

    core = lax.rem(lax.axis_index("gx"), 2)
    core_arg = core.astype(jnp.int32).reshape(1)
    fields = jnp.concatenate([order_param[None], density[None], velocity])
    def along(value, axis, to):
        return lax.ppermute(value, axis, [(i, to(i) % lax.axis_size(axis)) for i in range(lax.axis_size(axis))])

    def swap(i):
        return i ^ 1

    other = along(fields, "gx", swap)
    far = along(fields, "gx", lambda i: i ^ 2)
    near, edge = vmem_call(gather_pair, [(5, 8, BY, LANES), (8, BY, LANES)])(core_arg, fields, other)
    near_edge = send(edge, lambda x, y, z: (x ^ 1, y, z + 1 if x & 1 else z - 1))
    far_edge = send(edge, lambda x, y, z: (x ^ 3, y, z + 1 if x & 1 else z - 1))
    far_again, near_edge, far_edge = lax.optimization_barrier((far, near_edge, far_edge))
    other_far = along(far_again, "gx", swap)
    pack, last_rows, first_rows = vmem_call(merge_edges, [(4, NX, BY, LANES), (8, 24, LANES), (8, 24, LANES)])(
        core_arg, near, far_again, other_far, near_edge, far_edge
    )
    low = along(pack, "gy", lambda i: i + 1)
    high = along(pack, "gy", lambda i: i - 1)
    low2 = along(last_rows, "gy", lambda i: i + 2)
    high2 = along(first_rows, "gy", lambda i: i - 2)
    mine, away = make_steps()(core_arg, pack, low, high, low2, high2)
    back = along(away, "gx", swap)
    return tuple(vmem_call(join_halves, [(4, BY, LANES), (19, 4, BY, LANES)])(core_arg, mine, back))


def solution(mesh):
    return jax.shard_map(
        on_device,
        mesh=mesh,
        in_specs=(P("gx", "gy", "gz"), P("gx", "gy", "gz"), P(None, "gx", "gy", "gz")),
        out_specs=(P("gx", "gy", "gz"), P(None, "gx", "gy", "gz")),
        check_vma=False,
    )
```

```python
import jax
import jax.numpy as jnp
from jax import lax
from jax.experimental import pallas as pl
from jax.experimental.pallas import tpu as pltpu
from jax.sharding import PartitionSpec as P

ITERS = 5
DIRECTIONS = [
    (0, 0, 0),
    (1, 0, 0),
    (-1, 0, 0),
    (0, 1, 0),
    (0, -1, 0),
    (0, 0, 1),
    (0, 0, -1),
    (1, 1, 0),
    (-1, -1, 0),
    (1, -1, 0),
    (-1, 1, 0),
    (1, 0, 1),
    (-1, 0, -1),
    (1, 0, -1),
    (-1, 0, 1),
    (0, 1, 1),
    (0, -1, -1),
    (0, 1, -1),
    (0, -1, 1),
]
INDEX = {c: i for i, c in enumerate(DIRECTIONS)}
quadratic = -0.1
quartic = 0.1
stiffness = 0.02
mobility = 0.5

AXES = ("gx", "gy", "gz")
F32 = jnp.float32
NX = 16
BY = 16
LANES = 128
EDGE = 20
PART = 26
GAP = 24
ROWS = 72
OWN = 30


def tiles(radius):
    return [OWN - radius + 8 * k for k in range(-(-(BY + 2 * radius) // 8))]


def lane_masks(core, shape):
    lane = lax.broadcasted_iota(jnp.int32, shape, len(shape) - 1)
    low, high = lane < EDGE, lane >= LANES - EDGE
    first = core == 0
    send = (first & low) | (jnp.logical_not(first) & high)
    take = (first & high) | (jnp.logical_not(first) & low)
    return send, take


def gather_pair(core_ref, mine_ref, other_ref, both_ref, edge_ref):
    core = core_ref[0]
    lo, hi = core * 4, 4 - core * 4
    send, _ = lane_masks(core, (BY, LANES))
    for source, base in ((mine_ref, lo), (other_ref, hi)):
        for x in range(4):
            packed = None
            for f in range(5):
                value = source[f, x]
                both_ref[f, base + x] = value
                part = jnp.where(send, value, 0.0)
                part = pltpu.roll(part, GAP * f, 1) if f else part
                packed = part if packed is None else packed + part
            edge_ref[base + x] = packed


def unpack_edge(edge, f):
    return pltpu.roll(edge, LANES - GAP * f, 1) if f else edge


def spare_lanes(core, shape):
    lane = lax.broadcasted_iota(jnp.int32, shape, len(shape) - 1)
    start = jnp.where(core == 0, 82, 18)
    return (lane >= start) & (lane < start + PART), lane, start


def merge_edges(core_ref, near_ref, far_ref, other_ref, near_edge, far_edge, pack_ref, up_ref, down_ref):
    core = core_ref[0]
    lo, hi = core * 4, 4 - core * 4
    _, take = lane_masks(core, (BY, LANES))
    spare, _, _ = spare_lanes(core, (BY, LANES))
    for n in range(NX):
        if n < 8:
            source, k, x, edge = near_ref, n, n, near_edge[n]
            pack_ref[4, n] = edge
        else:
            source, k, base = (far_ref, n - 8, lo) if n < 12 else (other_ref, n - 12, hi)
            x = base + 8 + n % 4
            edge = far_edge[x - 8]
        pair, row = (x // 2, (x % 2) * 12) if n < 8 else (lax.div(base, 2) + 4 + n % 4 // 2, (n % 2) * 12)
        order = None
        for f in range(5):
            value = jnp.where(take, unpack_edge(edge, f), source[f, k])
            if f == 0:
                order = value
            elif n >= 8:
                pack_ref[f - 1, x - 8] = jnp.where(spare, pltpu.roll(order, LANES - PART * f, 1), value)
            count = 4 if f == 0 else 2
            up_ref[pair, row : row + count, :] = value[BY - count :]
            down_ref[pair, row : row + count, :] = value[:count]
            row += count


def prev_lane(v):
    return pltpu.roll(v, 1, 1)


def next_lane(v):
    return pltpu.roll(v, LANES - 1, 1)


def collide(density, vel, kick, old):
    moved = [v + g for v, g in zip(vel, kick)]
    pairs = ((0, 1), (0, 2), (1, 2))
    if old is None:
        unit = density * (1.0 / 36.0)
        rest = unit
        drift = moved
        square = [m * m for m in moved]
        cross = [moved[d] * moved[e] for d, e in pairs]
    else:
        unit = density * (-4.0 / 36.0)
        rest = density * (-5.0 / 36.0)
        drift = [1.25 * v + g for v, g in zip(vel, kick)]
        square = [v * b + g * m for v, g, b, m in zip(vel, kick, drift, moved)]
        cross = [vel[d] * drift[e] + kick[d] * moved[e] for d, e in pairs]
    unit3 = unit * 3.0
    unit45 = unit * 4.5
    unit9 = unit * 9.0
    sq = [unit45 * v for v in square]
    cr = [unit9 * v for v in cross]
    dr = [unit3 * v for v in drift]
    base = rest - (1.0 / 3.0) * (sq[0] + sq[1] + sq[2])

    def settle(i, value):
        return value if old is None else value + old(i)

    post = {0: settle(0, 12.0 * base)}
    axis = [base + v for v in sq]
    for d in range(3):
        even = 2.0 * axis[d]
        odd = 2.0 * dr[d]
        c = [0, 0, 0]
        c[d] = 1
        i = INDEX[tuple(c)]
        post[i] = settle(i, even + odd)
        c[d] = -1
        i = INDEX[tuple(c)]
        post[i] = settle(i, even - odd)
    for k, (d, e) in enumerate(pairs):
        even = axis[d] + sq[e]
        for sign in (1, -1):
            part = even + cr[k] if sign == 1 else even - cr[k]
            odd = dr[d] + dr[e] if sign == 1 else dr[d] - dr[e]
            c = [0, 0, 0]
            c[d], c[e] = 1, sign
            i = INDEX[tuple(c)]
            post[i] = settle(i, part + odd)
            c[d], c[e] = -1, -sign
            i = INDEX[tuple(c)]
            post[i] = settle(i, part - odd)
    return post


def moments(f):
    both, diff = {}, {}
    for i in range(1, 19, 2):
        both[i] = f[i] + f[i + 1]
        diff[i] = f[i] - f[i + 1]
    rho = ((f[0] + both[1]) + (both[3] + both[5])) + (
        ((both[7] + both[9]) + (both[11] + both[13])) + (both[15] + both[17])
    )
    mx = (diff[1] + (diff[7] + diff[9])) + (diff[11] + diff[13])
    my = (diff[3] + (diff[7] - diff[9])) + (diff[15] + diff[17])
    mz = (diff[5] + (diff[11] - diff[13])) + (diff[15] - diff[17])
    return rho, (mx, my, mz)


class Passes:
    def __init__(self, pops, order, chem, rho, inv, vel):
        self.pops, self.orders, self.chems, self.rho, self.inv, self.vel = pops, order, chem, rho, inv, vel

    def run(self, first, count, names, offset=None, unroll=1):
        behind = {"collide": 0, "flow": -3, "order": -6, "chem": 3}

        def body(n, _):
            for name, step in names:
                shift = behind[name] - 12 * step if offset is None else offset
                x = (n + shift) & (NX - 1)
                getattr(self, name)(step, x, (x + 1) & (NX - 1), (x - 1) & (NX - 1))
            return 0

        lax.fori_loop(first, first + count, body, 0, unroll=unroll)

    def left(self, step):
        return 4 * (ITERS - 1 - step)

    def chem(self, step, x, up, down):
        order, chem = self.orders[step % 2], self.chems[step % 2]
        for r in tiles(self.left(step) + 3):
            here = order[x, pl.ds(r, 8), :]
            beside = (order[up, pl.ds(r, 8), :] + order[down, pl.ds(r, 8), :]) + (
                order[x, pl.ds(r + 1, 8), :] + order[x, pl.ds(r - 1, 8), :]
            )
            beside = beside + (next_lane(here) + prev_lane(here))
            chem[x, pl.ds(r, 8), :] = here * ((quadratic + 6.0 * stiffness) + quartic * (here * here)) - stiffness * beside

    def collide(self, step, x, up, down):
        order, chem = self.orders[step % 2], self.chems[step % 2]
        was = (step - 1) % 2
        rho, inv, vel, old, new = self.rho[was], self.inv[was], self.vel[was], self.pops[was], self.pops[1 - was]
        to = {0: x, 1: up, -1: down}
        for r in tiles(self.left(step) + 2):
            at = pl.ds(r, 8)
            mu = chem[x, at, :]
            density = rho[x, at, :]
            inverse = 1.0 / density if step == 0 else inv[x, at, :]
            pull = ((-0.5 * (-4.0) ** max(step - 1, 0)) * order[x, at, :]) * inverse
            kick = [
                pull * (chem[up, at, :] - chem[down, at, :]),
                pull * (chem[x, pl.ds(r + 1, 8), :] - chem[x, pl.ds(r - 1, 8), :]),
                pull * (next_lane(mu) - prev_lane(mu)),
            ]
            before = None if step == 0 else (lambda i: old[i, x, at, :])
            post = collide(density, [vel[d, x, at, :] for d in range(3)], kick, before)
            for i in range(19):
                cx, cy, cz = DIRECTIONS[i]
                value = post[i]
                if cz:
                    value = prev_lane(value) if cz == 1 else next_lane(value)
                new[i, to[cx], pl.ds(r + cy, 8), :] = value

    def flow(self, step, x, up, down):
        now = step % 2
        for r in tiles(self.left(step) + 1):
            at = pl.ds(r, 8)
            total, moms = moments([self.pops[now][i, x, at, :] for i in range(19)])
            inverse = 1.0 / total
            self.rho[now][x, at, :] = total
            self.inv[now][x, at, :] = inverse
            for d in range(3):
                self.vel[now][d, x, at, :] = moms[d] * inverse

    def order(self, step, x, up, down):
        now = step % 2
        order, chem, vel = self.orders[now], self.chems[now], self.vel[now]
        for r in tiles(self.left(step)):
            at, north, south = pl.ds(r, 8), pl.ds(r + 1, 8), pl.ds(r - 1, 8)
            here = order[x, at, :]
            mu = chem[x, at, :]
            ux, uy, uz = (vel[d, x, at, :] for d in range(3))
            total = (ux + vel[0, up, at, :]) * (here + order[up, at, :])
            total = total - (ux + vel[0, down, at, :]) * (here + order[down, at, :])
            total = total + (uy + vel[1, x, north, :]) * (here + order[x, north, :])
            total = total - (uy + vel[1, x, south, :]) * (here + order[x, south, :])
            spread = (chem[up, at, :] + chem[down, at, :]) + (chem[x, north, :] + chem[x, south, :]) - 4.0 * mu
            face = (0.25 * (uz + next_lane(uz))) * (here + next_lane(here)) - mobility * (next_lane(mu) - mu)
            self.orders[1 - now][x, at, :] = here - ((0.25 * total - mobility * spread) + (face - prev_lane(face)))


def steps_kernel(core_ref, near, own, low_mine, low_other, low, high_mine, high_other, high, low2, high2, mine_ref, send_ref, pops_a, pops_b, order_a, order_b, chem_a, chem_b, rho_a, rho_b, inv_a, inv_b, vel_a, vel_b):
    core = core_ref[0]

    targets = (order_a, rho_b, vel_b.at[0], vel_b.at[1], vel_b.at[2])
    _, lane, start = spare_lanes(core, (BY, LANES))
    source_lane = lax.rem(lane - start + 2 * LANES - PART, LANES)

    _, take = lane_masks(core, (BY, LANES))
    lo, hi = core * 4, 4 - core * 4
    blocks = (
        (((near, 0, 0), (near, 4, 4)), own, OWN),
        (((low_mine, 0, lo), (low_other, 0, hi)), low, OWN - 16),
        (((high_mine, 0, lo), (high_other, 0, hi)), high, OWN + 16),
    )

    def load_block(k, _):
        for sources, pack, row in blocks:
            for source, skip, base in sources:
                x = base + k
                edge = pack[4, x]
                for f, target in enumerate(targets):
                    target[x, pl.ds(row, 16), :] = jnp.where(take, unpack_edge(edge, f), source[f, skip + k])
            for x in (k, k + 4):
                order = None
                for f in range(1, 5):
                    value = pack[f - 1, x]
                    targets[f][x + 8, pl.ds(row, 16), :] = value
                    moved = pltpu.roll(value, PART * f, 1)
                    order = moved if order is None else jnp.where(source_lane >= PART * (f - 1), moved, order)
                order_a[x + 8, pl.ds(row, 16), :] = order
        return 0

    lax.fori_loop(0, 4, load_block, 0)

    def load(pair, _):
        for half in range(2):
            x = 2 * pair + half
            for f, target in enumerate(targets):
                count, row = (4, 12 * half) if f == 0 else (2, 12 * half + 2 + 2 * f)
                target[x, pl.ds(OWN - 16 - count, count), :] = low2[pair, row : row + count, :]
                target[x, pl.ds(OWN + 32, count), :] = high2[pair, row : row + count, :]
        return 0

    lax.fori_loop(0, NX // 2, load, 0)

    passes = Passes((pops_a, pops_b), (order_a, order_b), (chem_a, chem_b), (rho_a, rho_b), (inv_a, inv_b), (vel_a, vel_b))
    run = passes.run
    run(0, NX, [("chem", 0)], offset=0, unroll=4)
    for step in range(ITERS - 1):
        start = 16 * step
        early = step > 0
        run(start, 4, [("collide", step)] + [("chem", step), ("order", step - 1), ("flow", step - 1)] * early)
        run(start + 4, 4, [("flow", step), ("collide", step)] + [("chem", step), ("order", step - 1)] * early)
        run(start + 8, 4, [("order", step), ("flow", step), ("collide", step)] + [("chem", step)] * early)
        run(start + 12, 4, [("chem", step + 1), ("order", step), ("flow", step), ("collide", step)])
    step = ITERS - 1
    start = 16 * step
    run(start, 4, [("collide", step), ("chem", step), ("order", step - 1), ("flow", step - 1)])
    run(start + 4, 4, [("flow", step), ("collide", step), ("chem", step), ("order", step - 1)])
    run(start + 8, 2, [("flow", step), ("collide", step), ("chem", step)])
    run(start + 10, 2, [("chem", step)], unroll=2)
    run(14, 2, [("collide", step)], offset=0, unroll=2)
    run(7, 2, [("flow", step)], offset=0, unroll=2)
    run(15, 2, [("flow", step)], offset=0, unroll=2)
    run(0, 8, [("order", step)], offset=0, unroll=4)
    pops = (pops_a, pops_b)[step % 2]
    order = (order_a, order_b)[ITERS % 2]

    keep = kept_lanes(core, (BY, LANES))
    for x in range(4):
        for i in range(20):
            source, scale = (order, None) if i == 19 else (pops.at[i], 1.0 / 256.0)
            here = source[core * 4 + x, pl.ds(OWN, 16), :]
            mine_ref[i, x] = here if scale is None else here * scale
            there = source[4 - core * 4 + x, pl.ds(OWN, 16), :]
            there = there if scale is None else there * scale
            if i % 2 == 0:
                first = there
            else:
                send_ref[i // 2, x] = jnp.where(keep, first, pltpu.roll(there, LANES // 2, 1))


def kept_lanes(core, shape):
    lane = lax.broadcasted_iota(jnp.int32, shape, len(shape) - 1)
    first = core == 0
    return (first & (lane < LANES // 2)) | (jnp.logical_not(first) & (lane >= LANES // 2))


def join_halves(core_ref, mine_ref, back_ref, order_ref, pops_ref):
    keep = kept_lanes(core_ref[0], (BY, LANES))
    for x in range(4):
        for i in range(20):
            back = back_ref[i // 2, x]
            value = jnp.where(keep, mine_ref[i, x], pltpu.roll(back, LANES // 2, 1) if i % 2 else back)
            if i == 19:
                order_ref[x] = value
            else:
                pops_ref[i, x] = value


def vmem_call(kernel, outs, scratch=(), limit=None):
    space = pl.BlockSpec(memory_space=pltpu.VMEM)

    def call(core, *args):
        return pl.pallas_call(
            kernel,
            out_shape=[jax.ShapeDtypeStruct(s, F32) for s in outs],
            in_specs=[pl.BlockSpec(memory_space=pltpu.SMEM)] + [space] * len(args),
            out_specs=[space] * len(outs),
            scratch_shapes=[pltpu.VMEM(s, F32) for s in scratch],
            compiler_params=pltpu.CompilerParams(vmem_limit_bytes=limit or 24 << 20),
        )(core, *args)

    return call


def make_steps():
    field = (NX, ROWS, LANES)
    return vmem_call(
        steps_kernel,
        [(20, 4, BY, LANES), (10, 4, BY, LANES)],
        [(19,) + field] * 2 + [field] * 8 + [(3,) + field] * 2,
        40 << 20,
    )


def on_device(order_param, density, velocity):
    sizes = [lax.axis_size(a) for a in AXES]

    def send(value, to):
        pairs = []
        for x in range(sizes[0]):
            for y in range(sizes[1]):
                for z in range(sizes[2]):
                    tx, ty, tz = to(x, y, z)
                    there = (tx % sizes[0] * sizes[1] + ty % sizes[1]) * sizes[2] + tz % sizes[2]
                    pairs.append(((x * sizes[1] + y) * sizes[2] + z, there))
        return lax.ppermute(value, AXES, pairs)

    core = lax.rem(lax.axis_index("gx"), 2)
    core_arg = core.astype(jnp.int32).reshape(1)
    fields = jnp.concatenate([order_param[None], density[None], velocity])
    def along(value, axis, to):
        return lax.ppermute(value, axis, [(i, to(i) % lax.axis_size(axis)) for i in range(lax.axis_size(axis))])

    def swap(i):
        return i ^ 1

    other = along(fields, "gx", swap)
    far = along(fields, "gx", lambda i: i ^ 2)
    near, edge = vmem_call(gather_pair, [(5, 8, BY, LANES), (8, BY, LANES)])(core_arg, fields, other)
    near_edge = send(edge, lambda x, y, z: (x ^ 1, y, z + 1 if x & 1 else z - 1))
    far_edge = send(edge, lambda x, y, z: (x ^ 3, y, z + 1 if x & 1 else z - 1))
    fields_again, _ = lax.optimization_barrier((fields, edge))
    low_mine = along(fields_again, "gy", lambda i: i + 1)
    high_mine = along(fields_again, "gy", lambda i: i - 1)
    far_again, near_edge, far_edge = lax.optimization_barrier((far, near_edge, far_edge))
    other_far = along(far_again, "gx", swap)
    other_far, low_mine, high_mine = lax.optimization_barrier((other_far, low_mine, high_mine))
    pack, last_rows, first_rows = vmem_call(merge_edges, [(5, 8, BY, LANES), (8, 24, LANES), (8, 24, LANES)])(
        core_arg, near, far_again, other_far, near_edge, far_edge
    )
    low = along(pack, "gy", lambda i: i + 1)
    high = along(pack, "gy", lambda i: i - 1)
    low_other = along(low_mine, "gx", swap)
    high_other = along(high_mine, "gx", swap)
    last_rows, first_rows, low_other, high_other = lax.optimization_barrier((last_rows, first_rows, low_other, high_other))
    low2 = along(last_rows, "gy", lambda i: i + 2)
    high2 = along(first_rows, "gy", lambda i: i - 2)
    mine, away = make_steps()(
        core_arg, near, pack, low_mine, low_other, low, high_mine, high_other, high, low2, high2
    )
    back = along(away, "gx", swap)
    return tuple(vmem_call(join_halves, [(4, BY, LANES), (19, 4, BY, LANES)])(core_arg, mine, back))


def solution(mesh):
    return jax.shard_map(
        on_device,
        mesh=mesh,
        in_specs=(P("gx", "gy", "gz"), P("gx", "gy", "gz"), P(None, "gx", "gy", "gz")),
        out_specs=(P("gx", "gy", "gz"), P(None, "gx", "gy", "gz")),
        check_vma=False,
    )
```

```python
import jax
import jax.numpy as jnp
from jax import lax
from jax.experimental import pallas as pl
from jax.experimental.pallas import tpu as pltpu
from jax.sharding import PartitionSpec as P

ITERS = 5
DIRECTIONS = [
    (0, 0, 0),
    (1, 0, 0),
    (-1, 0, 0),
    (0, 1, 0),
    (0, -1, 0),
    (0, 0, 1),
    (0, 0, -1),
    (1, 1, 0),
    (-1, -1, 0),
    (1, -1, 0),
    (-1, 1, 0),
    (1, 0, 1),
    (-1, 0, -1),
    (1, 0, -1),
    (-1, 0, 1),
    (0, 1, 1),
    (0, -1, -1),
    (0, 1, -1),
    (0, -1, 1),
]
INDEX = {c: i for i, c in enumerate(DIRECTIONS)}
quadratic = -0.1
quartic = 0.1
stiffness = 0.02
mobility = 0.5

AXES = ("gx", "gy", "gz")
F32 = jnp.float32
NX = 16
BY = 16
LANES = 128
EDGE = 20
HALF = 40
PART = 26
GAP = 24
ROWS = 72
OWN = 30


def tiles(radius):
    return [OWN - radius + 8 * k for k in range(-(-(BY + 2 * radius) // 8))]


def lane_masks(core, shape):
    lane = lax.broadcasted_iota(jnp.int32, shape, len(shape) - 1)
    low, high = lane < EDGE, lane >= LANES - EDGE
    first = core == 0
    send = (first & low) | (jnp.logical_not(first) & high)
    take = (first & high) | (jnp.logical_not(first) & low)
    return send, take


def gather_pair(core_ref, mine_ref, other_ref, both_ref, edge_ref):
    core = core_ref[0]
    lo, hi = core * 4, 4 - core * 4
    send, _ = lane_masks(core, (BY, LANES))
    for source, base in ((mine_ref, lo), (other_ref, hi)):
        for x in range(4):
            packed = None
            for f in range(5):
                value = source[f, x]
                both_ref[f, base + x] = value
                part = jnp.where(send, value, 0.0)
                part = pltpu.roll(part, GAP * f, 1) if f else part
                packed = part if packed is None else packed + part
            edge_ref[base + x] = packed


def unpack_edge(edge, f):
    return pltpu.roll(edge, LANES - GAP * f, 1) if f else edge


def far_row_lanes(core, shape):
    lane = lax.broadcasted_iota(jnp.int32, shape, len(shape) - 1)
    spare = jnp.where(core == 0, 76, 12)
    own = jnp.where(core == 0, 120, 56)
    return (lane >= spare) & (lane < spare + HALF), lax.rem(lane - own + LANES, LANES) < HALF


def spare_lanes(core, shape):
    lane = lax.broadcasted_iota(jnp.int32, shape, len(shape) - 1)
    start = jnp.where(core == 0, 82, 18)
    return (lane >= start) & (lane < start + PART), lane, start


def merge_edges(core_ref, near_ref, far_ref, other_ref, near_edge, far_edge, pack_ref, up_ref, down_ref):
    core = core_ref[0]
    lo, hi = core * 4, 4 - core * 4
    _, take = lane_masks(core, (BY, LANES))
    spare, _, _ = spare_lanes(core, (BY, LANES))
    travel, _ = far_row_lanes(core, (2, LANES))
    for n in range(NX):
        if n < 8:
            source, k, x, edge = near_ref, n, n, near_edge[n]
            pack_ref[4, n] = edge
        else:
            source, k, base = (far_ref, n - 8, lo) if n < 12 else (other_ref, n - 12, hi)
            x = base + 8 + n % 4
            edge = far_edge[x - 8]
        order = None
        for f in range(5):
            value = jnp.where(take, unpack_edge(edge, f), source[f, k])
            if f == 0:
                order = value
            elif n >= 8:
                pack_ref[f - 1, x - 8] = jnp.where(spare, pltpu.roll(order, LANES - PART * f, 1), value)
            if f > 0:
                two, shift = (f - 1) // 2 * 2, LANES - 44 - HALF * ((f - 1) % 2)
                for target, rows, first in ((up_ref, value[BY - 2 :], BY - 4 + two), (down_ref, value[:2], two)):
                    part = pltpu.roll(order[first : first + 2], shift, 1)
                    target[x, 2 * f - 2 : 2 * f, :] = jnp.where(travel, part, rows)


def prev_lane(v):
    return pltpu.roll(v, 1, 1)


def next_lane(v):
    return pltpu.roll(v, LANES - 1, 1)


def collide(density, vel, kick, old):
    moved = [v + g for v, g in zip(vel, kick)]
    pairs = ((0, 1), (0, 2), (1, 2))
    if old is None:
        unit = density * (1.0 / 36.0)
        rest = unit
        drift = moved
        square = [m * m for m in moved]
        cross = [moved[d] * moved[e] for d, e in pairs]
    else:
        unit = density * (-4.0 / 36.0)
        rest = density * (-5.0 / 36.0)
        drift = [1.25 * v + g for v, g in zip(vel, kick)]
        square = [v * b + g * m for v, g, b, m in zip(vel, kick, drift, moved)]
        cross = [vel[d] * drift[e] + kick[d] * moved[e] for d, e in pairs]
    unit3 = unit * 3.0
    unit45 = unit * 4.5
    unit9 = unit * 9.0
    sq = [unit45 * v for v in square]
    cr = [unit9 * v for v in cross]
    dr = [unit3 * v for v in drift]
    base = rest - (1.0 / 3.0) * (sq[0] + sq[1] + sq[2])

    def settle(i, value):
        return value if old is None else value + old(i)

    post = {0: settle(0, 12.0 * base)}
    axis = [base + v for v in sq]
    for d in range(3):
        even = 2.0 * axis[d]
        odd = 2.0 * dr[d]
        c = [0, 0, 0]
        c[d] = 1
        i = INDEX[tuple(c)]
        post[i] = settle(i, even + odd)
        c[d] = -1
        i = INDEX[tuple(c)]
        post[i] = settle(i, even - odd)
    for k, (d, e) in enumerate(pairs):
        even = axis[d] + sq[e]
        for sign in (1, -1):
            part = even + cr[k] if sign == 1 else even - cr[k]
            odd = dr[d] + dr[e] if sign == 1 else dr[d] - dr[e]
            c = [0, 0, 0]
            c[d], c[e] = 1, sign
            i = INDEX[tuple(c)]
            post[i] = settle(i, part + odd)
            c[d], c[e] = -1, -sign
            i = INDEX[tuple(c)]
            post[i] = settle(i, part - odd)
    return post


def moments(f):
    both, diff = {}, {}
    for i in range(1, 19, 2):
        both[i] = f[i] + f[i + 1]
        diff[i] = f[i] - f[i + 1]
    rho = ((f[0] + both[1]) + (both[3] + both[5])) + (
        ((both[7] + both[9]) + (both[11] + both[13])) + (both[15] + both[17])
    )
    mx = (diff[1] + (diff[7] + diff[9])) + (diff[11] + diff[13])
    my = (diff[3] + (diff[7] - diff[9])) + (diff[15] + diff[17])
    mz = (diff[5] + (diff[11] - diff[13])) + (diff[15] - diff[17])
    return rho, (mx, my, mz)


class Passes:
    def __init__(self, pops, order, chem, rho, inv, vel):
        self.pops, self.orders, self.chems, self.rho, self.inv, self.vel = pops, order, chem, rho, inv, vel

    def run(self, first, count, names, offset=None, unroll=1):
        behind = {"collide": 0, "flow": -3, "order": -6, "chem": 3}

        def body(n, _):
            for name, step in names:
                shift = behind[name] - 12 * step if offset is None else offset
                x = (n + shift) & (NX - 1)
                getattr(self, name)(step, x, (x + 1) & (NX - 1), (x - 1) & (NX - 1))
            return 0

        lax.fori_loop(first, first + count, body, 0, unroll=unroll)

    def left(self, step):
        return 4 * (ITERS - 1 - step)

    def chem(self, step, x, up, down):
        order, chem = self.orders[step % 2], self.chems[step % 2]
        for r in tiles(self.left(step) + 3):
            here = order[x, pl.ds(r, 8), :]
            beside = (order[up, pl.ds(r, 8), :] + order[down, pl.ds(r, 8), :]) + (
                order[x, pl.ds(r + 1, 8), :] + order[x, pl.ds(r - 1, 8), :]
            )
            beside = beside + (next_lane(here) + prev_lane(here))
            chem[x, pl.ds(r, 8), :] = here * ((quadratic + 6.0 * stiffness) + quartic * (here * here)) - stiffness * beside

    def collide(self, step, x, up, down):
        order, chem = self.orders[step % 2], self.chems[step % 2]
        was = (step - 1) % 2
        rho, inv, vel, old, new = self.rho[was], self.inv[was], self.vel[was], self.pops[was], self.pops[1 - was]
        to = {0: x, 1: up, -1: down}
        for r in tiles(self.left(step) + 2):
            at = pl.ds(r, 8)
            mu = chem[x, at, :]
            density = rho[x, at, :]
            inverse = 1.0 / density if step == 0 else inv[x, at, :]
            pull = ((-0.5 * (-4.0) ** max(step - 1, 0)) * order[x, at, :]) * inverse
            kick = [
                pull * (chem[up, at, :] - chem[down, at, :]),
                pull * (chem[x, pl.ds(r + 1, 8), :] - chem[x, pl.ds(r - 1, 8), :]),
                pull * (next_lane(mu) - prev_lane(mu)),
            ]
            before = None if step == 0 else (lambda i: old[i, x, at, :])
            post = collide(density, [vel[d, x, at, :] for d in range(3)], kick, before)
            for i in range(19):
                cx, cy, cz = DIRECTIONS[i]
                value = post[i]
                if cz:
                    value = prev_lane(value) if cz == 1 else next_lane(value)
                new[i, to[cx], pl.ds(r + cy, 8), :] = value

    def flow(self, step, x, up, down):
        now = step % 2
        for r in tiles(self.left(step) + 1):
            at = pl.ds(r, 8)
            total, moms = moments([self.pops[now][i, x, at, :] for i in range(19)])
            inverse = 1.0 / total
            self.rho[now][x, at, :] = total
            self.inv[now][x, at, :] = inverse
            for d in range(3):
                self.vel[now][d, x, at, :] = moms[d] * inverse

    def order(self, step, x, up, down):
        now = step % 2
        order, chem, vel = self.orders[now], self.chems[now], self.vel[now]
        for r in tiles(self.left(step)):
            at, north, south = pl.ds(r, 8), pl.ds(r + 1, 8), pl.ds(r - 1, 8)
            here = order[x, at, :]
            mu = chem[x, at, :]
            ux, uy, uz = (vel[d, x, at, :] for d in range(3))
            total = (ux + vel[0, up, at, :]) * (here + order[up, at, :])
            total = total - (ux + vel[0, down, at, :]) * (here + order[down, at, :])
            total = total + (uy + vel[1, x, north, :]) * (here + order[x, north, :])
            total = total - (uy + vel[1, x, south, :]) * (here + order[x, south, :])
            spread = (chem[up, at, :] + chem[down, at, :]) + (chem[x, north, :] + chem[x, south, :]) - 4.0 * mu
            face = (0.25 * (uz + next_lane(uz))) * (here + next_lane(here)) - mobility * (next_lane(mu) - mu)
            self.orders[1 - now][x, at, :] = here - ((0.25 * total - mobility * spread) + (face - prev_lane(face)))


def steps_kernel(core_ref, near, own, low_mine, low_other, low, high_mine, high_other, high, low2, high2, mine_ref, send_ref, pops_a, pops_b, order_a, order_b, chem_a, chem_b, rho_a, rho_b, inv_a, inv_b, vel_a, vel_b):
    core = core_ref[0]

    targets = (order_a, rho_b, vel_b.at[0], vel_b.at[1], vel_b.at[2])
    _, lane, start = spare_lanes(core, (BY, LANES))
    source_lane = lax.rem(lane - start + 2 * LANES - PART, LANES)

    _, take = lane_masks(core, (BY, LANES))
    lo, hi = core * 4, 4 - core * 4
    blocks = (
        (((near, 0, 0), (near, 4, 4)), own, OWN),
        (((low_mine, 0, lo), (low_other, 0, hi)), low, OWN - 16),
        (((high_mine, 0, lo), (high_other, 0, hi)), high, OWN + 16),
    )

    def load_block(k, _):
        for sources, pack, row in blocks:
            for source, skip, base in sources:
                x = base + k
                edge = pack[4, x]
                for f, target in enumerate(targets):
                    target[x, pl.ds(row, 16), :] = jnp.where(take, unpack_edge(edge, f), source[f, skip + k])
            for x in (k, k + 4):
                order = None
                for f in range(1, 5):
                    value = pack[f - 1, x]
                    targets[f][x + 8, pl.ds(row, 16), :] = value
                    moved = pltpu.roll(value, PART * f, 1)
                    order = moved if order is None else jnp.where(source_lane >= PART * (f - 1), moved, order)
                order_a[x + 8, pl.ds(row, 16), :] = order
        return 0

    lax.fori_loop(0, 4, load_block, 0)

    _, first_half = far_row_lanes(core, (2, LANES))

    def load(pair, _):
        for half in range(2):
            x = 2 * pair + half
            for source, order_row, row in ((low2, OWN - 20, OWN - 18), (high2, OWN + 32, OWN + 32)):
                rows = [source[x, 2 * k : 2 * k + 2, :] for k in range(4)]
                for f in range(1, 5):
                    targets[f][x, pl.ds(row, 2), :] = rows[f - 1]
                for k in (0, 2):
                    both = jnp.where(first_half, pltpu.roll(rows[k], 44, 1), pltpu.roll(rows[k + 1], 44 + HALF, 1))
                    order_a[x, pl.ds(order_row + k, 2), :] = both
        return 0

    lax.fori_loop(0, NX // 2, load, 0)

    passes = Passes((pops_a, pops_b), (order_a, order_b), (chem_a, chem_b), (rho_a, rho_b), (inv_a, inv_b), (vel_a, vel_b))
    run = passes.run
    run(0, NX, [("chem", 0)], offset=0, unroll=4)
    for step in range(ITERS - 1):
        start = 16 * step
        early = step > 0
        run(start, 4, [("collide", step)] + [("chem", step), ("order", step - 1), ("flow", step - 1)] * early)
        run(start + 4, 4, [("flow", step), ("collide", step)] + [("chem", step), ("order", step - 1)] * early)
        run(start + 8, 4, [("order", step), ("flow", step), ("collide", step)] + [("chem", step)] * early)
        run(start + 12, 4, [("chem", step + 1), ("order", step), ("flow", step), ("collide", step)])
    step = ITERS - 1
    start = 16 * step
    run(start, 4, [("collide", step), ("chem", step), ("order", step - 1), ("flow", step - 1)])
    run(start + 4, 4, [("flow", step), ("collide", step), ("chem", step), ("order", step - 1)])
    run(start + 8, 2, [("flow", step), ("collide", step), ("chem", step)])
    run(start + 10, 2, [("chem", step)], unroll=2)
    run(14, 2, [("collide", step)], offset=0, unroll=2)
    run(7, 2, [("flow", step)], offset=0, unroll=2)
    run(15, 2, [("flow", step)], offset=0, unroll=2)
    run(0, 8, [("order", step)], offset=0, unroll=4)
    pops = (pops_a, pops_b)[step % 2]
    order = (order_a, order_b)[ITERS % 2]

    keep = kept_lanes(core, (BY, LANES))
    for x in range(4):
        for i in range(20):
            source, scale = (order, None) if i == 19 else (pops.at[i], 1.0 / 256.0)
            here = source[core * 4 + x, pl.ds(OWN, 16), :]
            mine_ref[i, x] = here if scale is None else here * scale
            there = source[4 - core * 4 + x, pl.ds(OWN, 16), :]
            there = there if scale is None else there * scale
            if i % 2 == 0:
                first = there
            else:
                send_ref[i // 2, x] = jnp.where(keep, first, pltpu.roll(there, LANES // 2, 1))


def kept_lanes(core, shape):
    lane = lax.broadcasted_iota(jnp.int32, shape, len(shape) - 1)
    first = core == 0
    return (first & (lane < LANES // 2)) | (jnp.logical_not(first) & (lane >= LANES // 2))


def join_halves(core_ref, mine_ref, back_ref, order_ref, pops_ref):
    keep = kept_lanes(core_ref[0], (BY, LANES))
    for x in range(4):
        for i in range(20):
            back = back_ref[i // 2, x]
            value = jnp.where(keep, mine_ref[i, x], pltpu.roll(back, LANES // 2, 1) if i % 2 else back)
            if i == 19:
                order_ref[x] = value
            else:
                pops_ref[i, x] = value


def vmem_call(kernel, outs, scratch=(), limit=None):
    space = pl.BlockSpec(memory_space=pltpu.VMEM)

    def call(core, *args):
        return pl.pallas_call(
            kernel,
            out_shape=[jax.ShapeDtypeStruct(s, F32) for s in outs],
            in_specs=[pl.BlockSpec(memory_space=pltpu.SMEM)] + [space] * len(args),
            out_specs=[space] * len(outs),
            scratch_shapes=[pltpu.VMEM(s, F32) for s in scratch],
            compiler_params=pltpu.CompilerParams(vmem_limit_bytes=limit or 24 << 20),
        )(core, *args)

    return call


def make_steps():
    field = (NX, ROWS, LANES)
    return vmem_call(
        steps_kernel,
        [(20, 4, BY, LANES), (10, 4, BY, LANES)],
        [(19,) + field] * 2 + [field] * 8 + [(3,) + field] * 2,
        40 << 20,
    )


def on_device(order_param, density, velocity):
    sizes = [lax.axis_size(a) for a in AXES]

    def send(value, to):
        pairs = []
        for x in range(sizes[0]):
            for y in range(sizes[1]):
                for z in range(sizes[2]):
                    tx, ty, tz = to(x, y, z)
                    there = (tx % sizes[0] * sizes[1] + ty % sizes[1]) * sizes[2] + tz % sizes[2]
                    pairs.append(((x * sizes[1] + y) * sizes[2] + z, there))
        return lax.ppermute(value, AXES, pairs)

    core = lax.rem(lax.axis_index("gx"), 2)
    core_arg = core.astype(jnp.int32).reshape(1)
    fields = jnp.concatenate([order_param[None], density[None], velocity])
    def along(value, axis, to):
        return lax.ppermute(value, axis, [(i, to(i) % lax.axis_size(axis)) for i in range(lax.axis_size(axis))])

    def swap(i):
        return i ^ 1

    other = along(fields, "gx", swap)
    far = along(fields, "gx", lambda i: i ^ 2)
    near, edge = vmem_call(gather_pair, [(5, 8, BY, LANES), (8, BY, LANES)])(core_arg, fields, other)
    near_edge = send(edge, lambda x, y, z: (x ^ 1, y, z + 1 if x & 1 else z - 1))
    far_edge = send(edge, lambda x, y, z: (x ^ 3, y, z + 1 if x & 1 else z - 1))
    fields_again, _ = lax.optimization_barrier((fields, edge))
    low_mine = along(fields_again, "gy", lambda i: i + 1)
    high_mine = along(fields_again, "gy", lambda i: i - 1)
    far_again, near_edge, far_edge = lax.optimization_barrier((far, near_edge, far_edge))
    other_far = along(far_again, "gx", swap)
    other_far, low_mine, high_mine = lax.optimization_barrier((other_far, low_mine, high_mine))
    pack, last_rows, first_rows = vmem_call(merge_edges, [(5, 8, BY, LANES), (NX, 8, LANES), (NX, 8, LANES)])(
        core_arg, near, far_again, other_far, near_edge, far_edge
    )
    low = along(pack, "gy", lambda i: i + 1)
    high = along(pack, "gy", lambda i: i - 1)
    low_other = along(low_mine, "gx", swap)
    high_other = along(high_mine, "gx", swap)
    last_rows, first_rows, low_other, high_other = lax.optimization_barrier((last_rows, first_rows, low_other, high_other))
    low2 = along(last_rows, "gy", lambda i: i + 2)
    high2 = along(first_rows, "gy", lambda i: i - 2)
    mine, away = make_steps()(
        core_arg, near, pack, low_mine, low_other, low, high_mine, high_other, high, low2, high2
    )
    back = along(away, "gx", swap)
    return tuple(vmem_call(join_halves, [(4, BY, LANES), (19, 4, BY, LANES)])(core_arg, mine, back))


def solution(mesh):
    return jax.shard_map(
        on_device,
        mesh=mesh,
        in_specs=(P("gx", "gy", "gz"), P("gx", "gy", "gz"), P(None, "gx", "gy", "gz")),
        out_specs=(P("gx", "gy", "gz"), P(None, "gx", "gy", "gz")),
        check_vma=False,
    )
```

```python
import jax
import jax.numpy as jnp
from jax import lax
from jax.experimental import pallas as pl
from jax.experimental.pallas import tpu as pltpu
from jax.sharding import PartitionSpec as P

ITERS = 5
DIRECTIONS = [
    (0, 0, 0),
    (1, 0, 0),
    (-1, 0, 0),
    (0, 1, 0),
    (0, -1, 0),
    (0, 0, 1),
    (0, 0, -1),
    (1, 1, 0),
    (-1, -1, 0),
    (1, -1, 0),
    (-1, 1, 0),
    (1, 0, 1),
    (-1, 0, -1),
    (1, 0, -1),
    (-1, 0, 1),
    (0, 1, 1),
    (0, -1, -1),
    (0, 1, -1),
    (0, -1, 1),
]
INDEX = {c: i for i, c in enumerate(DIRECTIONS)}
quadratic = -0.1
quartic = 0.1
stiffness = 0.02
mobility = 0.5

AXES = ("gx", "gy", "gz")
F32 = jnp.float32
NX = 16
BY = 16
LANES = 128
EDGE = 20
HALF = 40
PART = 26
GAP = 24
ROWS = 72
OWN = 30


def tiles(radius):
    return [OWN - radius + 8 * k for k in range(-(-(BY + 2 * radius) // 8))]


def lane_masks(core, shape):
    lane = lax.broadcasted_iota(jnp.int32, shape, len(shape) - 1)
    low, high = lane < EDGE, lane >= LANES - EDGE
    first = core == 0
    send = (first & low) | (jnp.logical_not(first) & high)
    take = (first & high) | (jnp.logical_not(first) & low)
    return send, take


def gather_pair(core_ref, mine_ref, other_ref, both_ref, edge_ref):
    core = core_ref[0]
    lo, hi = core * 4, 4 - core * 4
    send, _ = lane_masks(core, (BY, LANES))
    for source, base in ((mine_ref, lo), (other_ref, hi)):
        for x in range(4):
            packed = None
            for f in range(5):
                value = source[f, x]
                both_ref[f, base + x] = value
                part = jnp.where(send, value, 0.0)
                part = pltpu.roll(part, GAP * f, 1) if f else part
                packed = part if packed is None else packed + part
            edge_ref[base + x] = packed


def unpack_edge(edge, f):
    return pltpu.roll(edge, LANES - GAP * f, 1) if f else edge


def far_row_lanes(core, shape):
    lane = lax.broadcasted_iota(jnp.int32, shape, len(shape) - 1)
    spare = jnp.where(core == 0, 76, 12)
    own = jnp.where(core == 0, 120, 56)
    return (lane >= spare) & (lane < spare + HALF), lax.rem(lane - own + LANES, LANES) < HALF


def spare_lanes(core, shape):
    lane = lax.broadcasted_iota(jnp.int32, shape, len(shape) - 1)
    start = jnp.where(core == 0, 82, 18)
    return (lane >= start) & (lane < start + PART), lane, start


def merge_edges(core_ref, near_ref, far_ref, other_ref, near_edge, far_edge, pack_ref, up_ref, down_ref):
    core = core_ref[0]
    lo, hi = core * 4, 4 - core * 4
    _, take = lane_masks(core, (BY, LANES))
    spare, _, _ = spare_lanes(core, (BY, LANES))
    travel, _ = far_row_lanes(core, (2, LANES))
    for n in range(NX):
        if n < 8:
            source, k, x, edge = near_ref, n, n, near_edge[n]
            pack_ref[4, n] = edge
        else:
            source, k, base = (far_ref, n - 8, lo) if n < 12 else (other_ref, n - 12, hi)
            x = base + 8 + n % 4
            edge = far_edge[x - 8]
        order = None
        for f in range(5):
            value = jnp.where(take, unpack_edge(edge, f), source[f, k])
            if f == 0:
                order = value
            elif n >= 8:
                pack_ref[f - 1, x - 8] = jnp.where(spare, pltpu.roll(order, LANES - PART * f, 1), value)
            if f > 0:
                two, shift = (f - 1) // 2 * 2, LANES - 44 - HALF * ((f - 1) % 2)
                for target, rows, first in ((up_ref, value[BY - 2 :], BY - 4 + two), (down_ref, value[:2], two)):
                    part = pltpu.roll(order[first : first + 2], shift, 1)
                    target[x, 2 * f - 2 : 2 * f, :] = jnp.where(travel, part, rows)


def prev_lane(v):
    return pltpu.roll(v, 1, 1)


def next_lane(v):
    return pltpu.roll(v, LANES - 1, 1)


def collide(density, vel, kick, old):
    moved = [v + g for v, g in zip(vel, kick)]
    pairs = ((0, 1), (0, 2), (1, 2))
    if old is None:
        unit = density * (1.0 / 36.0)
        rest = unit
        drift = moved
        square = [m * m for m in moved]
        cross = [moved[d] * moved[e] for d, e in pairs]
    else:
        unit = density * (-4.0 / 36.0)
        rest = density * (-5.0 / 36.0)
        drift = [1.25 * v + g for v, g in zip(vel, kick)]
        square = [v * b + g * m for v, g, b, m in zip(vel, kick, drift, moved)]
        cross = [vel[d] * drift[e] + kick[d] * moved[e] for d, e in pairs]
    unit3 = unit * 3.0
    unit45 = unit * 4.5
    unit9 = unit * 9.0
    sq = [unit45 * v for v in square]
    cr = [unit9 * v for v in cross]
    dr = [unit3 * v for v in drift]
    base = rest - (1.0 / 3.0) * (sq[0] + sq[1] + sq[2])

    def settle(i, value):
        return value if old is None else value + old(i)

    post = {0: settle(0, 12.0 * base)}
    axis = [base + v for v in sq]
    for d in range(3):
        even = 2.0 * axis[d]
        odd = 2.0 * dr[d]
        c = [0, 0, 0]
        c[d] = 1
        i = INDEX[tuple(c)]
        post[i] = settle(i, even + odd)
        c[d] = -1
        i = INDEX[tuple(c)]
        post[i] = settle(i, even - odd)
    for k, (d, e) in enumerate(pairs):
        even = axis[d] + sq[e]
        for sign in (1, -1):
            part = even + cr[k] if sign == 1 else even - cr[k]
            odd = dr[d] + dr[e] if sign == 1 else dr[d] - dr[e]
            c = [0, 0, 0]
            c[d], c[e] = 1, sign
            i = INDEX[tuple(c)]
            post[i] = settle(i, part + odd)
            c[d], c[e] = -1, -sign
            i = INDEX[tuple(c)]
            post[i] = settle(i, part - odd)
    return post


def moments(f):
    both, diff = {}, {}
    for i in range(1, 19, 2):
        both[i] = f[i] + f[i + 1]
        diff[i] = f[i] - f[i + 1]
    rho = ((f[0] + both[1]) + (both[3] + both[5])) + (
        ((both[7] + both[9]) + (both[11] + both[13])) + (both[15] + both[17])
    )
    mx = (diff[1] + (diff[7] + diff[9])) + (diff[11] + diff[13])
    my = (diff[3] + (diff[7] - diff[9])) + (diff[15] + diff[17])
    mz = (diff[5] + (diff[11] - diff[13])) + (diff[15] - diff[17])
    return rho, (mx, my, mz)


class Passes:
    def __init__(self, pops, order, chem, rho, inv, vel, order_next, chem_next):
        self.pops, self.orders, self.chems, self.rho, self.inv, self.vel = pops, order, chem, rho, inv, vel
        self.order_next, self.chem_next = order_next, chem_next

    def run(self, first, count, names, offset=None, unroll=1):
        behind = {"collide": 0, "flow": -3, "order": -6, "chem": 3}

        def body(n, _):
            for name, step in names:
                shift = behind[name] - 12 * step if offset is None else offset
                x = (n + shift) & (NX - 1)
                getattr(self, name)(step, x, (x + 1) & (NX - 1), (x - 1) & (NX - 1))
            return 0

        lax.fori_loop(first, first + count, body, 0, unroll=unroll)

    def left(self, step):
        return 4 * (ITERS - 1 - step)

    def chem(self, step, x, up, down):
        order, chem = self.orders[step % 2], self.chems[step % 2]
        for r in tiles(self.left(step) + 3):
            here = order[x, pl.ds(r, 8), :]
            beside = (order[up, pl.ds(r, 8), :] + order[down, pl.ds(r, 8), :]) + (
                order[x, pl.ds(r + 1, 8), :] + order[x, pl.ds(r - 1, 8), :]
            )
            after = next_lane(here)
            self.order_next[step % 2][x, pl.ds(r, 8), :] = after
            beside = beside + (after + prev_lane(here))
            chem[x, pl.ds(r, 8), :] = here * ((quadratic + 6.0 * stiffness) + quartic * (here * here)) - stiffness * beside

    def collide(self, step, x, up, down):
        order, chem = self.orders[step % 2], self.chems[step % 2]
        was = (step - 1) % 2
        rho, inv, vel, old, new = self.rho[was], self.inv[was], self.vel[was], self.pops[was], self.pops[1 - was]
        to = {0: x, 1: up, -1: down}
        for r in tiles(self.left(step) + 2):
            at = pl.ds(r, 8)
            mu = chem[x, at, :]
            density = rho[x, at, :]
            inverse = 1.0 / density if step == 0 else inv[x, at, :]
            pull = ((-0.5 * (-4.0) ** max(step - 1, 0)) * order[x, at, :]) * inverse
            after = next_lane(mu)
            self.chem_next[step % 2][x, at, :] = after
            kick = [
                pull * (chem[up, at, :] - chem[down, at, :]),
                pull * (chem[x, pl.ds(r + 1, 8), :] - chem[x, pl.ds(r - 1, 8), :]),
                pull * (after - prev_lane(mu)),
            ]
            before = None if step == 0 else (lambda i: old[i, x, at, :])
            post = collide(density, [vel[d, x, at, :] for d in range(3)], kick, before)
            for i in range(19):
                cx, cy, cz = DIRECTIONS[i]
                value = post[i]
                if cz:
                    value = prev_lane(value) if cz == 1 else next_lane(value)
                new[i, to[cx], pl.ds(r + cy, 8), :] = value

    def flow(self, step, x, up, down):
        now = step % 2
        for r in tiles(self.left(step) + 1):
            at = pl.ds(r, 8)
            total, moms = moments([self.pops[now][i, x, at, :] for i in range(19)])
            inverse = 1.0 / total
            self.rho[now][x, at, :] = total
            self.inv[now][x, at, :] = inverse
            for d in range(3):
                self.vel[now][d, x, at, :] = moms[d] * inverse

    def order(self, step, x, up, down):
        now = step % 2
        order, chem, vel = self.orders[now], self.chems[now], self.vel[now]
        for r in tiles(self.left(step)):
            at, north, south = pl.ds(r, 8), pl.ds(r + 1, 8), pl.ds(r - 1, 8)
            here = order[x, at, :]
            mu = chem[x, at, :]
            ux, uy, uz = (vel[d, x, at, :] for d in range(3))
            total = (ux + vel[0, up, at, :]) * (here + order[up, at, :])
            total = total - (ux + vel[0, down, at, :]) * (here + order[down, at, :])
            total = total + (uy + vel[1, x, north, :]) * (here + order[x, north, :])
            total = total - (uy + vel[1, x, south, :]) * (here + order[x, south, :])
            spread = (chem[up, at, :] + chem[down, at, :]) + (chem[x, north, :] + chem[x, south, :]) - 4.0 * mu
            face = (0.25 * (uz + next_lane(uz))) * (here + self.order_next[now][x, at, :]) - mobility * (self.chem_next[now][x, at, :] - mu)
            self.orders[1 - now][x, at, :] = here - ((0.25 * total - mobility * spread) + (face - prev_lane(face)))


def steps_kernel(core_ref, near, own, low_mine, low_other, low, high_mine, high_other, high, low2, high2, mine_ref, send_ref, pops_a, pops_b, order_a, order_b, chem_a, chem_b, rho_a, rho_b, inv_a, inv_b, vel_a, vel_b, shift_a, shift_b, shift_c, shift_d):
    core = core_ref[0]

    targets = (order_a, rho_b, vel_b.at[0], vel_b.at[1], vel_b.at[2])
    _, lane, start = spare_lanes(core, (BY, LANES))
    source_lane = lax.rem(lane - start + 2 * LANES - PART, LANES)

    _, take = lane_masks(core, (BY, LANES))
    lo, hi = core * 4, 4 - core * 4
    blocks = (
        (((near, 0, 0), (near, 4, 4)), own, OWN),
        (((low_mine, 0, lo), (low_other, 0, hi)), low, OWN - 16),
        (((high_mine, 0, lo), (high_other, 0, hi)), high, OWN + 16),
    )

    def load_block(k, _):
        for sources, pack, row in blocks:
            for source, skip, base in sources:
                x = base + k
                edge = pack[4, x]
                for f, target in enumerate(targets):
                    target[x, pl.ds(row, 16), :] = jnp.where(take, unpack_edge(edge, f), source[f, skip + k])
            for x in (k, k + 4):
                order = None
                for f in range(1, 5):
                    value = pack[f - 1, x]
                    targets[f][x + 8, pl.ds(row, 16), :] = value
                    moved = pltpu.roll(value, PART * f, 1)
                    order = moved if order is None else jnp.where(source_lane >= PART * (f - 1), moved, order)
                order_a[x + 8, pl.ds(row, 16), :] = order
        return 0

    lax.fori_loop(0, 4, load_block, 0)

    _, first_half = far_row_lanes(core, (2, LANES))

    def load(pair, _):
        for half in range(2):
            x = 2 * pair + half
            for source, order_row, row in ((low2, OWN - 20, OWN - 18), (high2, OWN + 32, OWN + 32)):
                rows = [source[x, 2 * k : 2 * k + 2, :] for k in range(4)]
                for f in range(1, 5):
                    targets[f][x, pl.ds(row, 2), :] = rows[f - 1]
                for k in (0, 2):
                    both = jnp.where(first_half, pltpu.roll(rows[k], 44, 1), pltpu.roll(rows[k + 1], 44 + HALF, 1))
                    order_a[x, pl.ds(order_row + k, 2), :] = both
        return 0

    lax.fori_loop(0, NX // 2, load, 0)

    passes = Passes((pops_a, pops_b), (order_a, order_b), (chem_a, chem_b), (rho_a, rho_b), (inv_a, inv_b), (vel_a, vel_b), (shift_a, shift_b), (shift_c, shift_d))
    run = passes.run
    run(0, NX, [("chem", 0)], offset=0, unroll=4)
    for step in range(ITERS - 1):
        start = 16 * step
        early = step > 0
        run(start, 4, [("collide", step)] + [("chem", step), ("order", step - 1), ("flow", step - 1)] * early)
        run(start + 4, 4, [("flow", step), ("collide", step)] + [("chem", step), ("order", step - 1)] * early)
        run(start + 8, 4, [("order", step), ("flow", step), ("collide", step)] + [("chem", step)] * early)
        run(start + 12, 4, [("chem", step + 1), ("order", step), ("flow", step), ("collide", step)])
    step = ITERS - 1
    start = 16 * step
    run(start, 4, [("collide", step), ("chem", step), ("order", step - 1), ("flow", step - 1)])
    run(start + 4, 4, [("flow", step), ("collide", step), ("chem", step), ("order", step - 1)])
    run(start + 8, 2, [("flow", step), ("collide", step), ("chem", step)])
    run(start + 10, 2, [("chem", step)], unroll=2)
    run(14, 2, [("collide", step)], offset=0, unroll=2)
    run(7, 2, [("flow", step)], offset=0, unroll=2)
    run(15, 2, [("flow", step)], offset=0, unroll=2)
    run(0, 8, [("order", step)], offset=0, unroll=4)
    pops = (pops_a, pops_b)[step % 2]
    order = (order_a, order_b)[ITERS % 2]

    keep = kept_lanes(core, (BY, LANES))
    for x in range(4):
        for i in range(20):
            source, scale = (order, None) if i == 19 else (pops.at[i], 1.0 / 256.0)
            here = source[core * 4 + x, pl.ds(OWN, 16), :]
            mine_ref[i, x] = here if scale is None else here * scale
            there = source[4 - core * 4 + x, pl.ds(OWN, 16), :]
            there = there if scale is None else there * scale
            if i % 2 == 0:
                first = there
            else:
                send_ref[i // 2, x] = jnp.where(keep, first, pltpu.roll(there, LANES // 2, 1))


def kept_lanes(core, shape):
    lane = lax.broadcasted_iota(jnp.int32, shape, len(shape) - 1)
    first = core == 0
    return (first & (lane < LANES // 2)) | (jnp.logical_not(first) & (lane >= LANES // 2))


def join_halves(core_ref, mine_ref, back_ref, order_ref, pops_ref):
    keep = kept_lanes(core_ref[0], (BY, LANES))
    for x in range(4):
        for i in range(20):
            back = back_ref[i // 2, x]
            value = jnp.where(keep, mine_ref[i, x], pltpu.roll(back, LANES // 2, 1) if i % 2 else back)
            if i == 19:
                order_ref[x] = value
            else:
                pops_ref[i, x] = value


def vmem_call(kernel, outs, scratch=(), limit=None):
    space = pl.BlockSpec(memory_space=pltpu.VMEM)

    def call(core, *args):
        return pl.pallas_call(
            kernel,
            out_shape=[jax.ShapeDtypeStruct(s, F32) for s in outs],
            in_specs=[pl.BlockSpec(memory_space=pltpu.SMEM)] + [space] * len(args),
            out_specs=[space] * len(outs),
            scratch_shapes=[pltpu.VMEM(s, F32) for s in scratch],
            compiler_params=pltpu.CompilerParams(vmem_limit_bytes=limit or 24 << 20),
        )(core, *args)

    return call


def make_steps():
    field = (NX, ROWS, LANES)
    return vmem_call(
        steps_kernel,
        [(20, 4, BY, LANES), (10, 4, BY, LANES)],
        [(19,) + field] * 2 + [field] * 8 + [(3,) + field] * 2 + [field] * 4,
        40 << 20,
    )


def on_device(order_param, density, velocity):
    sizes = [lax.axis_size(a) for a in AXES]

    def send(value, to):
        pairs = []
        for x in range(sizes[0]):
            for y in range(sizes[1]):
                for z in range(sizes[2]):
                    tx, ty, tz = to(x, y, z)
                    there = (tx % sizes[0] * sizes[1] + ty % sizes[1]) * sizes[2] + tz % sizes[2]
                    pairs.append(((x * sizes[1] + y) * sizes[2] + z, there))
        return lax.ppermute(value, AXES, pairs)

    core = lax.rem(lax.axis_index("gx"), 2)
    core_arg = core.astype(jnp.int32).reshape(1)
    fields = jnp.concatenate([order_param[None], density[None], velocity])
    def along(value, axis, to):
        return lax.ppermute(value, axis, [(i, to(i) % lax.axis_size(axis)) for i in range(lax.axis_size(axis))])

    def swap(i):
        return i ^ 1

    other = along(fields, "gx", swap)
    far = along(fields, "gx", lambda i: i ^ 2)
    near, edge = vmem_call(gather_pair, [(5, 8, BY, LANES), (8, BY, LANES)])(core_arg, fields, other)
    near_edge = send(edge, lambda x, y, z: (x ^ 1, y, z + 1 if x & 1 else z - 1))
    far_edge = send(edge, lambda x, y, z: (x ^ 3, y, z + 1 if x & 1 else z - 1))
    fields_again, _ = lax.optimization_barrier((fields, edge))
    low_mine = along(fields_again, "gy", lambda i: i + 1)
    high_mine = along(fields_again, "gy", lambda i: i - 1)
    far_again, near_edge, far_edge = lax.optimization_barrier((far, near_edge, far_edge))
    other_far = along(far_again, "gx", swap)
    other_far, low_mine, high_mine = lax.optimization_barrier((other_far, low_mine, high_mine))
    pack, last_rows, first_rows = vmem_call(merge_edges, [(5, 8, BY, LANES), (NX, 8, LANES), (NX, 8, LANES)])(
        core_arg, near, far_again, other_far, near_edge, far_edge
    )
    low = along(pack, "gy", lambda i: i + 1)
    high = along(pack, "gy", lambda i: i - 1)
    low_other = along(low_mine, "gx", swap)
    high_other = along(high_mine, "gx", swap)
    last_rows, first_rows, low_other, high_other = lax.optimization_barrier((last_rows, first_rows, low_other, high_other))
    low2 = along(last_rows, "gy", lambda i: i + 2)
    high2 = along(first_rows, "gy", lambda i: i - 2)
    mine, away = make_steps()(
        core_arg, near, pack, low_mine, low_other, low, high_mine, high_other, high, low2, high2
    )
    back = along(away, "gx", swap)
    return tuple(vmem_call(join_halves, [(4, BY, LANES), (19, 4, BY, LANES)])(core_arg, mine, back))


def solution(mesh):
    return jax.shard_map(
        on_device,
        mesh=mesh,
        in_specs=(P("gx", "gy", "gz"), P("gx", "gy", "gz"), P(None, "gx", "gy", "gz")),
        out_specs=(P("gx", "gy", "gz"), P(None, "gx", "gy", "gz")),
        check_vma=False,
    )
```

```python
import jax
import jax.numpy as jnp
from jax import lax
from jax.experimental import pallas as pl
from jax.experimental.pallas import tpu as pltpu
from jax.sharding import PartitionSpec as P

ITERS = 5
DIRECTIONS = [
    (0, 0, 0),
    (1, 0, 0),
    (-1, 0, 0),
    (0, 1, 0),
    (0, -1, 0),
    (0, 0, 1),
    (0, 0, -1),
    (1, 1, 0),
    (-1, -1, 0),
    (1, -1, 0),
    (-1, 1, 0),
    (1, 0, 1),
    (-1, 0, -1),
    (1, 0, -1),
    (-1, 0, 1),
    (0, 1, 1),
    (0, -1, -1),
    (0, 1, -1),
    (0, -1, 1),
]
INDEX = {c: i for i, c in enumerate(DIRECTIONS)}
quadratic = -0.1
quartic = 0.1
stiffness = 0.02
mobility = 0.5

AXES = ("gx", "gy", "gz")
F32 = jnp.float32
NX = 16
BY = 16
LANES = 128
EDGE = 20
HALF = 40
PART = 26
GAP = 24
ROWS = 72
OWN = 30


def tiles(radius):
    return [OWN - radius + 8 * k for k in range(-(-(BY + 2 * radius) // 8))]


def lane_masks(core, shape):
    lane = lax.broadcasted_iota(jnp.int32, shape, len(shape) - 1)
    low, high = lane < EDGE, lane >= LANES - EDGE
    first = core == 0
    send = (first & low) | (jnp.logical_not(first) & high)
    take = (first & high) | (jnp.logical_not(first) & low)
    return send, take


def gather_pair(core_ref, mine_ref, other_ref, both_ref, edge_ref):
    core = core_ref[0]
    lo, hi = core * 4, 4 - core * 4
    send, _ = lane_masks(core, (BY, LANES))
    for source, base in ((mine_ref, lo), (other_ref, hi)):
        for x in range(4):
            packed = None
            for f in range(5):
                value = source[f, x]
                both_ref[f, base + x] = value
                part = jnp.where(send, value, 0.0)
                part = pltpu.roll(part, GAP * f, 1) if f else part
                packed = part if packed is None else packed + part
            edge_ref[base + x] = packed


def unpack_edge(edge, f):
    return pltpu.roll(edge, LANES - GAP * f, 1) if f else edge


def far_row_lanes(core, shape):
    lane = lax.broadcasted_iota(jnp.int32, shape, len(shape) - 1)
    spare = jnp.where(core == 0, 76, 12)
    own = jnp.where(core == 0, 120, 56)
    return (lane >= spare) & (lane < spare + HALF), lax.rem(lane - own + LANES, LANES) < HALF


def spare_lanes(core, shape):
    lane = lax.broadcasted_iota(jnp.int32, shape, len(shape) - 1)
    start = jnp.where(core == 0, 82, 18)
    return (lane >= start) & (lane < start + PART), lane, start


def merge_edges(core_ref, near_ref, far_ref, other_ref, near_edge, far_edge, pack_ref, up_ref, down_ref):
    core = core_ref[0]
    lo, hi = core * 4, 4 - core * 4
    _, take = lane_masks(core, (BY, LANES))
    spare, _, _ = spare_lanes(core, (BY, LANES))
    travel, _ = far_row_lanes(core, (2, LANES))
    for n in range(NX):
        if n < 8:
            source, k, x, edge = near_ref, n, n, near_edge[n]
            pack_ref[4, n] = edge
        else:
            source, k, base = (far_ref, n - 8, lo) if n < 12 else (other_ref, n - 12, hi)
            x = base + 8 + n % 4
            edge = far_edge[x - 8]
        order = None
        for f in range(5):
            value = jnp.where(take, unpack_edge(edge, f), source[f, k])
            if f == 0:
                order = value
            elif n >= 8:
                pack_ref[f - 1, x - 8] = jnp.where(spare, pltpu.roll(order, LANES - PART * f, 1), value)
            if f > 0:
                two, shift = (f - 1) // 2 * 2, LANES - 44 - HALF * ((f - 1) % 2)
                for target, rows, first in ((up_ref, value[BY - 2 :], BY - 4 + two), (down_ref, value[:2], two)):
                    part = pltpu.roll(order[first : first + 2], shift, 1)
                    target[x, 2 * f - 2 : 2 * f, :] = jnp.where(travel, part, rows)


def prev_lane(v):
    return pltpu.roll(v, 1, 1)


def next_lane(v):
    return pltpu.roll(v, LANES - 1, 1)


def collide(density, vel, kick, old):
    moved = [v + g for v, g in zip(vel, kick)]
    pairs = ((0, 1), (0, 2), (1, 2))
    if old is None:
        unit = density * (1.0 / 36.0)
        rest = unit
        drift = moved
        square = [m * m for m in moved]
        cross = [moved[d] * moved[e] for d, e in pairs]
    else:
        unit = density * (-4.0 / 36.0)
        rest = density * (-5.0 / 36.0)
        drift = [1.25 * v + g for v, g in zip(vel, kick)]
        square = [v * b + g * m for v, g, b, m in zip(vel, kick, drift, moved)]
        cross = [vel[d] * drift[e] + kick[d] * moved[e] for d, e in pairs]
    unit3 = unit * 3.0
    unit45 = unit * 4.5
    unit9 = unit * 9.0
    sq = [unit45 * v for v in square]
    cr = [unit9 * v for v in cross]
    dr = [unit3 * v for v in drift]
    base = rest - (1.0 / 3.0) * (sq[0] + sq[1] + sq[2])

    def settle(i, value):
        return value if old is None else value + old(i)

    post = {0: settle(0, 12.0 * base)}
    axis = [base + v for v in sq]
    for d in range(3):
        even = 2.0 * axis[d]
        odd = 2.0 * dr[d]
        c = [0, 0, 0]
        c[d] = 1
        i = INDEX[tuple(c)]
        post[i] = settle(i, even + odd)
        c[d] = -1
        i = INDEX[tuple(c)]
        post[i] = settle(i, even - odd)
    for k, (d, e) in enumerate(pairs):
        even = axis[d] + sq[e]
        for sign in (1, -1):
            part = even + cr[k] if sign == 1 else even - cr[k]
            odd = dr[d] + dr[e] if sign == 1 else dr[d] - dr[e]
            c = [0, 0, 0]
            c[d], c[e] = 1, sign
            i = INDEX[tuple(c)]
            post[i] = settle(i, part + odd)
            c[d], c[e] = -1, -sign
            i = INDEX[tuple(c)]
            post[i] = settle(i, part - odd)
    return post


def moments(f):
    both, diff = {}, {}
    for i in range(1, 19, 2):
        both[i] = f[i] + f[i + 1]
        diff[i] = f[i] - f[i + 1]
    rho = ((f[0] + both[1]) + (both[3] + both[5])) + (
        ((both[7] + both[9]) + (both[11] + both[13])) + (both[15] + both[17])
    )
    mx = (diff[1] + (diff[7] + diff[9])) + (diff[11] + diff[13])
    my = (diff[3] + (diff[7] - diff[9])) + (diff[15] + diff[17])
    mz = (diff[5] + (diff[11] - diff[13])) + (diff[15] - diff[17])
    return rho, (mx, my, mz)


class Passes:
    def __init__(self, pops, order, chem, rho, inv, vel, order_next, chem_next):
        self.pops, self.orders, self.chems, self.rho, self.inv, self.vel = pops, order, chem, rho, inv, vel
        self.order_next, self.chem_next = order_next, chem_next

    def run(self, first, count, names, offset=None, unroll=1):
        behind = {"collide": 0, "flow": -3, "order": -6, "chem": 3}

        def body(n, _):
            for name, step in names:
                shift = behind[name] - 12 * step if offset is None else offset
                x = (n + shift) & (NX - 1)
                getattr(self, name)(step, x, (x + 1) & (NX - 1), (x - 1) & (NX - 1))
            return 0

        lax.fori_loop(first, first + count, body, 0, unroll=unroll)

    def left(self, step):
        return 4 * (ITERS - 1 - step)

    def chem(self, step, x, up, down):
        order, chem = self.orders[step % 2], self.chems[step % 2]
        for r in tiles(self.left(step) + 3):
            here = order[x, pl.ds(r, 8), :]
            beside = (order[up, pl.ds(r, 8), :] + order[down, pl.ds(r, 8), :]) + (
                order[x, pl.ds(r + 1, 8), :] + order[x, pl.ds(r - 1, 8), :]
            )
            after = next_lane(here)
            self.order_next[step % 2][x, pl.ds(r, 8), :] = after
            beside = beside + (after + prev_lane(here))
            chem[x, pl.ds(r, 8), :] = here * ((quadratic + 6.0 * stiffness) + quartic * (here * here)) - stiffness * beside

    def collide(self, step, x, up, down):
        order, chem = self.orders[step % 2], self.chems[step % 2]
        was = (step - 1) % 2
        rho, inv, vel, old, new = self.rho[was], self.inv[was], self.vel[was], self.pops[was], self.pops[1 - was]
        to = {0: x, 1: up, -1: down}
        for r in tiles(self.left(step) + 2):
            at = pl.ds(r, 8)
            mu = chem[x, at, :]
            density = rho[x, at, :]
            inverse = 1.0 / density if step == 0 else inv[x, at, :]
            pull = ((-0.5 * (-4.0) ** max(step - 1, 0)) * order[x, at, :]) * inverse
            after = next_lane(mu)
            self.chem_next[step % 2][x, at, :] = after
            kick = [
                pull * (chem[up, at, :] - chem[down, at, :]),
                pull * (chem[x, pl.ds(r + 1, 8), :] - chem[x, pl.ds(r - 1, 8), :]),
                pull * (after - prev_lane(mu)),
            ]
            before = None if step == 0 else (lambda i: old[i, x, at, :])
            post = collide(density, [vel[d, x, at, :] for d in range(3)], kick, before)
            for i in range(19):
                cx, cy, cz = DIRECTIONS[i]
                value = post[i]
                if cz:
                    value = prev_lane(value) if cz == 1 else next_lane(value)
                new[i, to[cx], pl.ds(r + cy, 8), :] = value

    def flow(self, step, x, up, down):
        now = step % 2
        for r in tiles(self.left(step) + 1):
            at = pl.ds(r, 8)
            total, moms = moments([self.pops[now][i, x, at, :] for i in range(19)])
            inverse = 1.0 / total
            self.rho[now][x, at, :] = total
            self.inv[now][x, at, :] = inverse
            for d in range(3):
                self.vel[now][d, x, at, :] = moms[d] * inverse

    def order(self, step, x, up, down):
        now = step % 2
        order, chem, vel = self.orders[now], self.chems[now], self.vel[now]
        for r in tiles(self.left(step)):
            at, north, south = pl.ds(r, 8), pl.ds(r + 1, 8), pl.ds(r - 1, 8)
            here = order[x, at, :]
            mu = chem[x, at, :]
            ux, uy, uz = (vel[d, x, at, :] for d in range(3))
            total = (ux + vel[0, up, at, :]) * (here + order[up, at, :])
            total = total - (ux + vel[0, down, at, :]) * (here + order[down, at, :])
            total = total + (uy + vel[1, x, north, :]) * (here + order[x, north, :])
            total = total - (uy + vel[1, x, south, :]) * (here + order[x, south, :])
            spread = (chem[up, at, :] + chem[down, at, :]) + (chem[x, north, :] + chem[x, south, :]) - 4.0 * mu
            face = (0.25 * (uz + next_lane(uz))) * (here + self.order_next[now][x, at, :]) - mobility * (self.chem_next[now][x, at, :] - mu)
            self.orders[1 - now][x, at, :] = here - ((0.25 * total - mobility * spread) + (face - prev_lane(face)))


def steps_kernel(core_ref, near, own, low_mine, low_other, low, high_mine, high_other, high, low2, high2, mine_ref, send_ref, pops_a, pops_b, order_a, order_b, chem_a, chem_b, rho_a, rho_b, inv_a, inv_b, vel_a, vel_b, shift_a, shift_b, shift_c, shift_d):
    core = core_ref[0]

    targets = (order_a, rho_b, vel_b.at[0], vel_b.at[1], vel_b.at[2])
    _, lane, start = spare_lanes(core, (BY, LANES))
    source_lane = lax.rem(lane - start + 2 * LANES - PART, LANES)

    _, take = lane_masks(core, (BY, LANES))
    lo, hi = core * 4, 4 - core * 4
    blocks = (
        (((near, 0, 0), (near, 4, 4)), own, OWN),
        (((low_mine, 0, lo), (low_other, 0, hi)), low, OWN - 16),
        (((high_mine, 0, lo), (high_other, 0, hi)), high, OWN + 16),
    )

    def load_block(k, _):
        for sources, pack, row in blocks:
            for source, skip, base in sources:
                x = base + k
                edge = pack[4, x]
                for f, target in enumerate(targets):
                    target[x, pl.ds(row, 16), :] = jnp.where(take, unpack_edge(edge, f), source[f, skip + k])
            for x in (k, k + 4):
                order = None
                for f in range(1, 5):
                    value = pack[f - 1, x]
                    targets[f][x + 8, pl.ds(row, 16), :] = value
                    moved = pltpu.roll(value, PART * f, 1)
                    order = moved if order is None else jnp.where(source_lane >= PART * (f - 1), moved, order)
                order_a[x + 8, pl.ds(row, 16), :] = order
        return 0

    lax.fori_loop(0, 4, load_block, 0, unroll=2)

    _, first_half = far_row_lanes(core, (2, LANES))

    def load(pair, _):
        for half in range(2):
            x = 2 * pair + half
            for source, order_row, row in ((low2, OWN - 20, OWN - 18), (high2, OWN + 32, OWN + 32)):
                rows = [source[x, 2 * k : 2 * k + 2, :] for k in range(4)]
                for f in range(1, 5):
                    targets[f][x, pl.ds(row, 2), :] = rows[f - 1]
                for k in (0, 2):
                    both = jnp.where(first_half, pltpu.roll(rows[k], 44, 1), pltpu.roll(rows[k + 1], 44 + HALF, 1))
                    order_a[x, pl.ds(order_row + k, 2), :] = both
        return 0

    lax.fori_loop(0, NX // 2, load, 0, unroll=4)

    passes = Passes((pops_a, pops_b), (order_a, order_b), (chem_a, chem_b), (rho_a, rho_b), (inv_a, inv_b), (vel_a, vel_b), (shift_a, shift_b), (shift_c, shift_d))
    run = passes.run
    run(0, NX, [("chem", 0)], offset=0, unroll=4)
    for step in range(ITERS - 1):
        start = 16 * step
        early = step > 0
        run(start, 4, [("collide", step)] + [("chem", step), ("order", step - 1), ("flow", step - 1)] * early)
        run(start + 4, 4, [("flow", step), ("collide", step)] + [("chem", step), ("order", step - 1)] * early)
        run(start + 8, 4, [("order", step), ("flow", step), ("collide", step)] + [("chem", step)] * early)
        run(start + 12, 4, [("chem", step + 1), ("order", step), ("flow", step), ("collide", step)])
    step = ITERS - 1
    start = 16 * step
    run(start, 4, [("collide", step), ("chem", step), ("order", step - 1), ("flow", step - 1)])
    run(start + 4, 4, [("flow", step), ("collide", step), ("chem", step), ("order", step - 1)])
    run(start + 8, 2, [("flow", step), ("collide", step), ("chem", step)])
    run(start + 10, 2, [("chem", step)], unroll=2)
    run(14, 2, [("collide", step)], offset=0, unroll=2)
    run(7, 2, [("flow", step)], offset=0, unroll=2)
    run(15, 2, [("flow", step)], offset=0, unroll=2)
    run(0, 8, [("order", step)], offset=0, unroll=4)
    pops = (pops_a, pops_b)[step % 2]
    order = (order_a, order_b)[ITERS % 2]

    keep = kept_lanes(core, (BY, LANES))
    for x in range(4):
        for i in range(20):
            source, scale = (order, None) if i == 19 else (pops.at[i], 1.0 / 256.0)
            here = source[core * 4 + x, pl.ds(OWN, 16), :]
            mine_ref[i, x] = here if scale is None else here * scale
            there = source[4 - core * 4 + x, pl.ds(OWN, 16), :]
            there = there if scale is None else there * scale
            if i % 2 == 0:
                first = there
            else:
                send_ref[i // 2, x] = jnp.where(keep, first, pltpu.roll(there, LANES // 2, 1))


def kept_lanes(core, shape):
    lane = lax.broadcasted_iota(jnp.int32, shape, len(shape) - 1)
    first = core == 0
    return (first & (lane < LANES // 2)) | (jnp.logical_not(first) & (lane >= LANES // 2))


def join_halves(core_ref, mine_ref, back_ref, order_ref, pops_ref):
    keep = kept_lanes(core_ref[0], (BY, LANES))
    for x in range(4):
        for i in range(20):
            back = back_ref[i // 2, x]
            value = jnp.where(keep, mine_ref[i, x], pltpu.roll(back, LANES // 2, 1) if i % 2 else back)
            if i == 19:
                order_ref[x] = value
            else:
                pops_ref[i, x] = value


def vmem_call(kernel, outs, scratch=(), limit=None):
    space = pl.BlockSpec(memory_space=pltpu.VMEM)

    def call(core, *args):
        return pl.pallas_call(
            kernel,
            out_shape=[jax.ShapeDtypeStruct(s, F32) for s in outs],
            in_specs=[pl.BlockSpec(memory_space=pltpu.SMEM)] + [space] * len(args),
            out_specs=[space] * len(outs),
            scratch_shapes=[pltpu.VMEM(s, F32) for s in scratch],
            compiler_params=pltpu.CompilerParams(vmem_limit_bytes=limit or 24 << 20),
        )(core, *args)

    return call


def make_steps():
    field = (NX, ROWS, LANES)
    return vmem_call(
        steps_kernel,
        [(20, 4, BY, LANES), (10, 4, BY, LANES)],
        [(19,) + field] * 2 + [field] * 8 + [(3,) + field] * 2 + [field] * 4,
        40 << 20,
    )


def on_device(order_param, density, velocity):
    sizes = [lax.axis_size(a) for a in AXES]

    def send(value, to):
        pairs = []
        for x in range(sizes[0]):
            for y in range(sizes[1]):
                for z in range(sizes[2]):
                    tx, ty, tz = to(x, y, z)
                    there = (tx % sizes[0] * sizes[1] + ty % sizes[1]) * sizes[2] + tz % sizes[2]
                    pairs.append(((x * sizes[1] + y) * sizes[2] + z, there))
        return lax.ppermute(value, AXES, pairs)

    core = lax.rem(lax.axis_index("gx"), 2)
    core_arg = core.astype(jnp.int32).reshape(1)
    fields = jnp.concatenate([order_param[None], density[None], velocity])
    def along(value, axis, to):
        return lax.ppermute(value, axis, [(i, to(i) % lax.axis_size(axis)) for i in range(lax.axis_size(axis))])

    def swap(i):
        return i ^ 1

    other = along(fields, "gx", swap)
    far = along(fields, "gx", lambda i: i ^ 2)
    near, edge = vmem_call(gather_pair, [(5, 8, BY, LANES), (8, BY, LANES)])(core_arg, fields, other)
    near_edge = send(edge, lambda x, y, z: (x ^ 1, y, z + 1 if x & 1 else z - 1))
    far_edge = send(edge, lambda x, y, z: (x ^ 3, y, z + 1 if x & 1 else z - 1))
    fields_again, _ = lax.optimization_barrier((fields, edge))
    low_mine = along(fields_again, "gy", lambda i: i + 1)
    high_mine = along(fields_again, "gy", lambda i: i - 1)
    far_again, near_edge, far_edge = lax.optimization_barrier((far, near_edge, far_edge))
    other_far = along(far_again, "gx", swap)
    other_far, low_mine, high_mine = lax.optimization_barrier((other_far, low_mine, high_mine))
    pack, last_rows, first_rows = vmem_call(merge_edges, [(5, 8, BY, LANES), (NX, 8, LANES), (NX, 8, LANES)])(
        core_arg, near, far_again, other_far, near_edge, far_edge
    )
    low = along(pack, "gy", lambda i: i + 1)
    high = along(pack, "gy", lambda i: i - 1)
    low_other = along(low_mine, "gx", swap)
    high_other = along(high_mine, "gx", swap)
    last_rows, first_rows, low_other, high_other = lax.optimization_barrier((last_rows, first_rows, low_other, high_other))
    low2 = along(last_rows, "gy", lambda i: i + 2)
    high2 = along(first_rows, "gy", lambda i: i - 2)
    mine, away = make_steps()(
        core_arg, near, pack, low_mine, low_other, low, high_mine, high_other, high, low2, high2
    )
    back = along(away, "gx", swap)
    return tuple(vmem_call(join_halves, [(4, BY, LANES), (19, 4, BY, LANES)])(core_arg, mine, back))


def solution(mesh):
    return jax.shard_map(
        on_device,
        mesh=mesh,
        in_specs=(P("gx", "gy", "gz"), P("gx", "gy", "gz"), P(None, "gx", "gy", "gz")),
        out_specs=(P("gx", "gy", "gz"), P(None, "gx", "gy", "gz")),
        check_vma=False,
    )
```
